512 devices in a mesh: lat: 16 (over y_hi, z), lon: 32 (over x, y_lo, core).
Axes of the slice: x: 4, y: 8 (y_hi: 2, y_lo: 4; y = y_hi * 4 + y_lo), z: 8, core: 2. Of those that a mesh axis runs over, the one named last changes fastest.
Arguments:
- fields: float32 [1024, 1024, 256], P('lat', 'lon'), may hold values from -6 to 6
- land_sea: int32 [512, 512], P('lat', 'lon'), may hold values 0 or 1
- w_depth: float32 [3, 3, 256], replicated, may hold values from -2 to 2
- b_depth: float32 [256], replicated, may hold values from -3 to 3
- w_one: bfloat16 [3, 3, 256, 300], replicated, may hold values from -0.125 to 0.125
- b_one: float32 [300], replicated, may hold values from -3 to 3
- w_two: bfloat16 [3, 3, 300, 300], replicated, may hold values from -0.125 to 0.125
- b_two: float32 [300], replicated, may hold values from -3 to 3
Outputs:
- level_out: float32 [512, 512, 300], P('lat', 'lon')
The draws below stay inside these ranges and needn't reach their ends.
All inputs are finite; a program needn't handle non-finite values. No bound on the sum of `land_sea` on one device may be relied on, other than what follows from the above.
Results may differ from the reference program's by a relative error of at most 0.0035.
Values may be sent and summed in bfloat16 or wider, within the bound.
No kernel may reach another device: no remote copies, remote signals or barrier semaphores. Data moves between devices by JAX's collectives and lax.ppermute only.
A program may use at most 64 MiB of HBM per device.

```python
import jax
import jax.numpy as jnp
from jax import lax

IN_CH = 256
OUT_CH = 300
LAT_CELLS = 512
LON_CELLS = 512
HALF_LAT = 1024
HALF_LON = 1024


def place_ends(drawn, own_key, least, largest):
    place = [jax.random.randint(jax.random.fold_in(own_key, axis), (), 0, length) for axis, length in enumerate(drawn.shape)]
    widest = drawn.shape.index(max(drawn.shape))
    beside = place[:widest] + [(place[widest] + 1) % drawn.shape[widest]] + place[widest + 1:]
    return drawn.at[tuple(place)].set(least).at[tuple(beside)].set(largest)


def levels(key, dims, cuts, smallest, largest):
    level, own = 1.0, jax.random.fold_in(key, 6)
    for axis_at, shards_of in cuts:
        heights = jnp.exp(jax.random.uniform(jax.random.fold_in(own, axis_at), (shards_of,), jnp.float32, smallest / len(cuts), largest / len(cuts)))
        level = level * jnp.repeat(heights, dims[axis_at] // shards_of).reshape([-1 if axis == axis_at else 1 for axis in range(len(dims))])
    return level


def scatter_about(rng, shape, scale, bound, split=(), dtype=jnp.bfloat16):
    array = scale * jax.random.normal(rng, shape, jnp.float32)
    if split:
        array = array * levels(rng, shape, split, -0.22, 0.18)
    return jnp.clip(array, -bound, bound).astype(dtype)


def setup_inputs(seed: int = 0) -> dict:
    splits = jax.random.split(jax.random.key(seed), 9)
    fields = scatter_about(splits[0], (HALF_LAT, HALF_LON, IN_CH), 1.0, 6.0, ((0, 16), (1, 32)), jnp.float32)
    land_sea = place_ends((jax.random.randint(splits[1], (LAT_CELLS, LON_CELLS), 0, 10) < 7).astype(jnp.int32), jax.random.fold_in(splits[1], 1), 0, 1)
    w_depth = scatter_about(splits[2], (3, 3, IN_CH), 9 ** -0.5, 2.0, (), jnp.float32)
    b_depth = scatter_about(splits[3], (IN_CH,), 0.5, 3.0, (), jnp.float32)
    w_one = scatter_about(splits[4], (3, 3, IN_CH, OUT_CH), (9 * IN_CH) ** -0.5, 0.125)
    b_one = scatter_about(splits[5], (OUT_CH,), 0.5, 3.0, (), jnp.float32)
    w_two = scatter_about(splits[6], (3, 3, OUT_CH, OUT_CH), (9 * OUT_CH) ** -0.5, 0.125)
    b_two = scatter_about(splits[7], (OUT_CH,), 0.5, 3.0, (), jnp.float32)
    return dict(fields=fields, land_sea=land_sea, w_depth=w_depth, b_depth=b_depth, w_one=w_one, b_one=b_one, w_two=w_two, b_two=b_two)


def cycle_pad(field, reach):
    wide = jnp.concatenate([field[:, -reach:], field, field[:, :reach]], axis=1)
    return jnp.pad(wide, ((reach, reach), (0, 0), (0, 0)))


def dilated(field, kernel, bias, reach):
    rows, cols = field.shape[0], field.shape[1]
    ext = cycle_pad(field, reach).astype(jnp.float32)
    weights = kernel.astype(jnp.float32)
    total = jnp.zeros((rows, cols, kernel.shape[3]), jnp.float32) + bias
    for a in range(3):
        for b in range(3):
            piece = ext[a * reach:a * reach + rows, b * reach:b * reach + cols]
            total = total + jnp.einsum("ijc,cd->ijd", piece, weights[a, b], precision=lax.Precision.HIGHEST)
    return total


def reference(fields, land_sea, w_depth, b_depth, w_one, b_one, w_two, b_two):
    rows = fields.shape[0] // 2
    cols = fields.shape[1] // 2
    wide = jnp.concatenate([fields[:, -1:], fields], axis=1)
    padded = jnp.pad(wide, ((1, 0), (0, 0), (0, 0)))
    down = jnp.zeros((rows, cols, fields.shape[2]), jnp.float32) + b_depth
    for a in range(3):
        for b in range(3):
            down = down + padded[a:a + 2 * rows:2, b:b + 2 * cols:2] * w_depth[a, b]
    mask = land_sea.astype(jnp.float32)[:, :, None]
    down_bf = (down * mask).astype(jnp.bfloat16)
    hidden = jax.nn.gelu(dilated(down_bf, w_one, b_one, 4), approximate=False).astype(jnp.bfloat16)
    return jax.nn.gelu(dilated(hidden, w_two, b_two, 8), approximate=False) * mask
```

```python
import jax
import jax.numpy as jnp
from jax import lax
from jax.experimental import pallas as pl
from jax.experimental.pallas import tpu as pltpu
from jax.sharding import PartitionSpec as P

ROWS = 32
COLS = 16
HALO = 12
EXT_R = ROWS + 2 * HALO
EXT_C = COLS + 2 * HALO
HID_R = ROWS + 16
HID_C = COLS + 16
PACK = EXT_R * HALO
MASKED = 2.0**100
LIMIT = 2.0**90
F32 = jnp.float32
BF16 = jnp.bfloat16


def mask_column(mask_row, eye):
    return jnp.sum(jnp.where(eye, mask_row, 0), axis=1, keepdims=True)


def down_kernel(f_ref, ls_ref, wd_ref, bd_ref, own_ref, edge_ref, south_ref, north_ref, edge):
    last = lax.axis_index("lat") == lax.axis_size("lat") - 1
    chans = f_ref.shape[2]
    sub = lax.broadcasted_iota(jnp.int32, (COLS, chans), 0)
    first = sub == 0
    eye = lax.broadcasted_iota(jnp.int32, (COLS, COLS), 0) == lax.broadcasted_iota(
        jnp.int32, (COLS, COLS), 1
    )
    weight = [[wd_ref[a, b : b + 1, :] for b in range(3)] for a in range(3)]
    bias = bd_ref[...]

    def terms(r, a):
        even = f_ref[r, pl.ds(0, COLS, stride=2), :]
        odd = f_ref[r, pl.ds(1, COLS, stride=2), :]
        return even * weight[a][1] + odd * weight[a][2], odd * weight[a][0]

    def put(i, here, after, masked):
        moved = pltpu.roll(after, 1, 0)
        edge[pl.ds(i, 1), :] = moved[0:1, :]
        value = here + jnp.where(first, 0.0, moved)
        if masked is not None:
            keep = mask_column(ls_ref[pl.ds(i, 1), :], eye) != 0
            value = jnp.where(keep, value, masked)
        own_ref[i] = value.astype(BF16)

    edge[...] = jnp.zeros_like(edge)
    h1, p1 = terms(0, 1)
    h2, p2 = terms(1, 2)
    put(0, h1 + h2 + bias, p1 + p2, jnp.full((COLS, chans), MASKED, F32))
    holed = jnp.where(first, MASKED, 0.0)

    def row(i, _):
        h0, p0 = terms(2 * i - 1, 0)
        h1, p1 = terms(2 * i, 1)
        h2, p2 = terms(2 * i + 1, 2)
        put(i, h0 + h1 + h2 + bias, p0 + p1 + p2, holed)
        return 0

    lax.fori_loop(1, ROWS, row, 0)
    h0, p0 = terms(2 * ROWS - 1, 0)
    scale = jnp.where(last, 0.0, 1.0)
    put(ROWS, h0 * scale, p0 * scale, None)

    edge_ref[...] = edge[...].astype(BF16)
    south_ref[0 : HALO + 1] = own_ref[ROWS - HALO : ROWS + 1]
    south_ref[HALO + 1] = edge[ROWS - HALO : ROWS - HALO + 16, :].astype(BF16)
    north_ref[0:HALO] = own_ref[0:HALO]
    north_ref[HALO] = edge[0:16, :].astype(BF16)


def band_kernel(own_ref, edge_ref, n_ref, s_ref, band_ref, col_ref, east_ref, west_ref, te, tw, col):
    col[HALO : HALO + ROWS + 16] = edge_ref[...].astype(F32)
    n_edge = n_ref[HALO + 1].astype(F32)
    s_edge = s_ref[HALO].astype(F32)
    col[0:HALO] = n_edge[0:HALO]
    col[HALO : HALO + 1] += n_edge[HALO : HALO + 1]
    col[HALO + ROWS : HALO + ROWS + 1] += s_edge[0:1]
    col[HALO + ROWS + 1 : EXT_R] = s_edge[1:HALO]

    def put(r, value):
        band_ref[r] = value.astype(BF16)
        te[r * HALO : (r + 1) * HALO] = value[COLS - HALO :]
        tw[r * HALO : (r + 1) * HALO] = value[:HALO]

    for r in range(EXT_R):
        i = r - HALO
        if i < 0:
            put(r, n_ref[r].astype(F32))
        elif i == 0:
            put(r, own_ref[0].astype(F32) + n_ref[HALO].astype(F32))
        elif i < ROWS:
            put(r, own_ref[i].astype(F32))
        elif i == ROWS:
            put(r, own_ref[ROWS].astype(F32) + s_ref[0].astype(F32))
        else:
            put(r, s_ref[i - ROWS].astype(F32))
    te[PACK : PACK + 64] = col[...]
    col_ref[...] = col[...].astype(BF16)
    east_ref[...] = te[...].astype(BF16)
    west_ref[...] = tw[...].astype(BF16)


def gelu(x):
    return 0.5 * x * (1.0 + lax.erf(x * (0.5**0.5)))


def conv_kernel(
    band_ref, col_ref, w_ref, e_ref, ls_ref, w1_ref, b1_ref, w2_ref, b2_ref, out_ref,
    tw, te, col, ext, db, h0, h8,
):
    lat = lax.axis_index("lat")
    last = lax.axis_size("lat") - 1
    out_ch = b1_ref.shape[1]
    tw[...] = w_ref[...].astype(F32)
    te[...] = e_ref[...].astype(F32)
    col[...] = col_ref[...].astype(F32)

    for r in range(EXT_R):
        ext[r, 0:HALO] = tw[r * HALO : (r + 1) * HALO]
        ext[r, HALO : HALO + COLS] = band_ref[r].astype(F32)
        ext[r, HALO + COLS : EXT_C] = te[r * HALO : (r + 1) * HALO]
        ext[r, HALO : HALO + 1] += tw[PACK + r : PACK + r + 1]
        ext[r, HALO + COLS : HALO + COLS + 1] += col[r : r + 1]
    for r in range(EXT_R):
        for b in range(3):
            piece = ext[r, 4 * b : 4 * b + HID_C]
            db[b, r] = jnp.where(piece > LIMIT, 0.0, piece).astype(BF16)

    step = 8

    def first(k, _):
        r0 = pl.multiple_of(k * step, step)
        total = jnp.zeros((step * HID_C, out_ch), F32) + b1_ref[...]
        for a in range(3):
            for b in range(3):
                piece = db[b, pl.ds(r0 + 4 * a, step)].reshape(step * HID_C, -1)
                total = total + jnp.dot(piece, w1_ref[a, b], preferred_element_type=F32)
        inside = jnp.logical_and(
            jnp.logical_or(k > 0, lat > 0),
            jnp.logical_or(k < HID_R // step - 1, lat < last),
        )
        value = gelu(total) * jnp.where(inside, 1.0, 0.0)
        value = value.reshape(step, HID_C, out_ch)
        h0[pl.ds(r0, step)] = value.astype(BF16)
        h8[pl.ds(r0, step)] = value[:, 8:24].astype(BF16)
        return 0

    lax.fori_loop(0, HID_R // step, first, 0)

    eye = lax.broadcasted_iota(jnp.int32, (COLS, COLS), 0) == lax.broadcasted_iota(
        jnp.int32, (COLS, COLS), 1
    )
    half = 16
    for k in range(ROWS // half):
        total = jnp.zeros((half * COLS, out_ch), F32) + b2_ref[...]
        for a in range(3):
            for b in range(3):
                rows = pl.ds(k * half + 8 * a, half)
                if b == 0:
                    piece = h0[rows, 0:COLS]
                elif b == 1:
                    piece = h8[rows]
                else:
                    piece = h0[rows, COLS : 2 * COLS]
                piece = piece.reshape(half * COLS, out_ch)
                total = total + jnp.dot(piece, w2_ref[a, b], preferred_element_type=F32)
        value = gelu(total).reshape(half, COLS, out_ch)
        for i in range(half):
            keep = mask_column(ls_ref[k * half + i : k * half + i + 1, :], eye)
            out_ref[k * half + i] = value[i] * keep.astype(F32)


def line(axis, by):
    count = lax.axis_size(axis)
    return [(i, i + by) for i in range(count) if 0 <= i + by < count]


def ring(axis, by):
    count = lax.axis_size(axis)
    return [(i, (i + by) % count) for i in range(count)]


def on_device(fields, land_sea, w_depth, b_depth, w_one, b_one, w_two, b_two):
    chans = fields.shape[2]
    out_ch = w_one.shape[3]
    vmem = pl.BlockSpec(memory_space=pltpu.VMEM)

    def shape(*dims, dtype=BF16):
        return jax.ShapeDtypeStruct(dims, dtype)

    lanes = 128

    def part(*dims):
        zeros = (0,) * len(dims)
        return pl.BlockSpec((*dims, lanes), lambda c: (*zeros, c))

    own, edge, south, north = pl.pallas_call(
        down_kernel,
        grid=(chans // lanes,),
        out_shape=(
            shape(ROWS + 1, COLS, chans),
            shape(ROWS + 16, chans),
            shape(HALO + 2, COLS, chans),
            shape(HALO + 1, COLS, chans),
        ),
        in_specs=[
            part(2 * ROWS, 2 * COLS),
            pl.BlockSpec((ROWS, COLS), lambda c: (0, 0)),
            part(3, 3),
            part(1),
        ],
        out_specs=[
            part(ROWS + 1, COLS),
            part(ROWS + 16),
            part(HALO + 2, COLS),
            part(HALO + 1, COLS),
        ],
        scratch_shapes=[pltpu.VMEM((ROWS + 16, lanes), F32)],
        compiler_params=pltpu.CompilerParams(vmem_limit_bytes=16 << 20),
        name="down",
    )(fields, land_sea, w_depth, b_depth[None])

    from_north = lax.ppermute(south, "lat", line("lat", 1))
    from_south = lax.ppermute(north, "lat", line("lat", -1))

    band, col, east, west = pl.pallas_call(
        band_kernel,
        out_shape=(
            shape(EXT_R, COLS, chans),
            shape(64, chans),
            shape(PACK + 64, chans),
            shape(PACK, chans),
        ),
        in_specs=[vmem] * 4,
        out_specs=[vmem] * 4,
        scratch_shapes=[
            pltpu.VMEM((PACK + 64, chans), F32),
            pltpu.VMEM((PACK, chans), F32),
            pltpu.VMEM((64, chans), F32),
        ],
        compiler_params=pltpu.CompilerParams(vmem_limit_bytes=16 << 20),
        name="band",
    )(own, edge, from_north, from_south)

    from_west = lax.ppermute(east, "lon", ring("lon", 1))
    from_east = lax.ppermute(west, "lon", ring("lon", -1))

    return pl.pallas_call(
        conv_kernel,
        out_shape=shape(ROWS, COLS, out_ch, dtype=F32),
        in_specs=[vmem] * 9,
        out_specs=vmem,
        scratch_shapes=[
            pltpu.VMEM((PACK + 64, chans), F32),
            pltpu.VMEM((PACK, chans), F32),
            pltpu.VMEM((64, chans), F32),
            pltpu.VMEM((EXT_R, EXT_C, chans), F32),
            pltpu.VMEM((3, EXT_R, HID_C, chans), BF16),
            pltpu.VMEM((HID_R, HID_C, out_ch), BF16),
            pltpu.VMEM((HID_R, COLS, out_ch), BF16),
        ],
        compiler_params=pltpu.CompilerParams(vmem_limit_bytes=32 << 20),
        name="convolve",
    )(band, col, from_west, from_east, land_sea, w_one, b_one[None], w_two, b_two[None])


def solution(mesh):
    return jax.shard_map(
        on_device,
        mesh=mesh,
        in_specs=(P("lat", "lon", None), P("lat", "lon"), P(), P(), P(), P(), P(), P()),
        out_specs=P("lat", "lon", None),
        check_vma=False,
    )
```

```python
import jax
import jax.numpy as jnp
from jax import lax
from jax.experimental import pallas as pl
from jax.experimental.pallas import tpu as pltpu
from jax.sharding import PartitionSpec as P

ROWS = 32
COLS = 16
HALO = 12
GROUP = 4
SLABS = COLS // GROUP
HALO_SLABS = HALO // GROUP
OWN = ROWS * GROUP
EXT_R = ROWS + 2 * HALO
EXT = EXT_R * GROUP
HID = (ROWS + 16) * GROUP
HID_SLABS = (COLS + 16) // GROUP
EDGE = HALO * GROUP
LANES = 128
CHUNKS = 4
MASKED = 2.0**100
LIMIT = 2.0**90
F32 = jnp.float32
BF16 = jnp.bfloat16


def resolved(x):
    return jnp.where(x > LIMIT, 0.0, x)


def down_kernel(
    f_hbm, ls_hbm, wd_hbm, bd_hbm,
    own_ref, below_ref, edge_ref, keep_ref, pa_ref, pb_ref,
    f_ref, ls_ref, wd_ref, bd_ref, f_sem, sems, mask, patch, edge,
):
    lat = lax.axis_index("lat")
    last = lat == lax.axis_size("lat") - 1
    small = [
        pltpu.make_async_copy(src, dst, sems.at[k])
        for k, (src, dst) in enumerate(((ls_hbm, ls_ref), (wd_hbm, wd_ref), (bd_hbm, bd_ref)))
    ]
    for copy in small:
        copy.start()
    tall = 2 * ROWS // CHUNKS
    copies = {}
    for h in range(2):
        for k in range(CHUNKS):
            copies[h, k] = pltpu.make_async_copy(
                f_hbm.at[pl.ds(k * tall, tall), :, pl.ds(h * LANES, LANES)],
                f_ref.at[h, pl.ds(k * tall, tall)],
                f_sem.at[h, k],
            )
            copies[h, k].start()
    for copy in small:
        copy.wait()

    sea = ls_ref[...].astype(F32)
    for i in range(ROWS):
        mask[COLS * i : COLS * (i + 1)] = jnp.broadcast_to(sea[:, i : i + 1], (COLS, LANES))
    edge[...] = jnp.zeros_like(edge)

    first = lax.broadcasted_iota(jnp.int32, (COLS, LANES), 0) == 0
    holed = jnp.where(first, MASKED, 0.0)
    scale = jnp.where(last, 0.0, 1.0)
    for h in range(2):
        at = slice(h * LANES, (h + 1) * LANES)
        weight = [
            [jnp.broadcast_to(wd_ref[a, b : b + 1, at], (COLS, LANES)) for b in range(3)]
            for a in range(3)
        ]
        bias = jnp.broadcast_to(bd_ref[:, at], (COLS, LANES))
        for i in range(ROWS + 1):
            if i < ROWS and (2 * i) % tall == 0:
                copies[h, 2 * i // tall].wait()
            here, after = None, None
            for a in range(3):
                r = 2 * i - 1 + a
                if r < 0 or r >= 2 * ROWS:
                    continue
                even = f_ref[h, r, pl.ds(0, COLS, stride=2), :]
                odd = f_ref[h, r, pl.ds(1, COLS, stride=2), :]
                p = even * weight[a][1] + odd * weight[a][2]
                q = odd * weight[a][0]
                here = p if here is None else here + p
                after = q if after is None else after + q
            if i == ROWS:
                here, after = here * scale, after * scale
            else:
                here = here + bias
            moved = pltpu.roll(after, 1, 0)
            edge[i : i + 1, at] = moved[0:1]
            value = here + jnp.where(first, 0.0, moved)
            if i == ROWS:
                below_ref[:, at] = value.astype(BF16)
                continue
            kept = mask[COLS * i : COLS * (i + 1)]
            value = jnp.where(kept > 0.5, value, MASKED if i == 0 else holed)
            for q in range(SLABS):
                cells = slice(GROUP * i, GROUP * (i + 1))
                patch[q, cells, at] = value[GROUP * q : GROUP * (q + 1)]
                if h == 0:
                    keep_ref[q, cells] = kept[GROUP * q : GROUP * (q + 1)]

    own_ref[...] = patch[...].astype(BF16)
    edge_ref[...] = edge[...].astype(BF16)

    def write(south_ref, north_ref):
        for q in range(SLABS):
            south_ref[EDGE * q : EDGE * (q + 1)] = own_ref[q, OWN - EDGE : OWN]
            north_ref[EDGE * q : EDGE * (q + 1)] = own_ref[q, 0:EDGE]
        base = EDGE * SLABS
        south_ref[base : base + 16] = below_ref[...]
        south_ref[base + 16 : base + 32] = edge[ROWS - HALO : ROWS - HALO + 16].astype(BF16)
        north_ref[base : base + 16] = edge[0:16].astype(BF16)
        north_ref[base + 16 : base + 32] = jnp.zeros((16, 2 * LANES), BF16)

    even = lax.rem(lat, 2) == 0

    @pl.when(even)
    def _():
        write(pa_ref, pb_ref)

    @pl.when(jnp.logical_not(even))
    def _():
        write(pb_ref, pa_ref)


def band_kernel(
    own_ref, below_ref, edge_ref, ra_ref, rb_ref,
    band_ref, col_ref, pa_ref, pb_ref,
    north, south, tile, col,
):
    even_lat = lax.rem(lax.axis_index("lat"), 2) == 0
    even_lon = lax.rem(lax.axis_index("lon"), 2) == 0

    @pl.when(even_lat)
    def _():
        south[...] = ra_ref[...]
        north[...] = rb_ref[...]

    @pl.when(jnp.logical_not(even_lat))
    def _():
        north[...] = ra_ref[...]
        south[...] = rb_ref[...]

    base = EDGE * SLABS
    col[HALO : HALO + ROWS + 16] = edge_ref[...].astype(F32)
    n_edge = north[base + 16 : base + 32].astype(F32)
    s_edge = south[base : base + 16].astype(F32)
    col[0:HALO] = n_edge[0:HALO]
    col[HALO : HALO + 1] += n_edge[HALO : HALO + 1]
    col[HALO + ROWS : HALO + ROWS + 1] += s_edge[0:1]
    col[HALO + ROWS + 1 : EXT_R] = s_edge[1:HALO]
    col_ref[...] = col[...].astype(BF16)

    above = north[base : base + 16].astype(F32)
    below = below_ref[...].astype(F32)
    for q in range(SLABS):
        cells = slice(GROUP * q, GROUP * (q + 1))
        tile[0, q] = own_ref[q, 0:16].astype(F32)
        tile[1, q] = south[EDGE * q : EDGE * q + 16].astype(F32)
        tile[0, q, 0:GROUP] += above[cells]
        tile[1, q, 0:GROUP] += below[cells]
        top, bottom = tile[0, q], tile[1, q]
        if q > 0:
            top, bottom = resolved(top), resolved(bottom)
        band_ref[q, 0:EDGE] = north[EDGE * q : EDGE * (q + 1)]
        band_ref[q, EDGE : EDGE + 16] = top.astype(BF16)
        band_ref[q, EDGE + 16 : EDGE + OWN] = own_ref[q, 16:OWN]
        band_ref[q, EDGE + OWN : EDGE + OWN + 16] = bottom.astype(BF16)
        band_ref[q, EDGE + OWN + 16 : EXT] = south[EDGE * q + 16 : EDGE * (q + 1)]

    def write(east_ref, west_ref):
        for k in range(HALO_SLABS):
            east_ref[EXT * k : EXT * (k + 1)] = band_ref[SLABS - HALO_SLABS + k]
            west_ref[EXT * k : EXT * (k + 1)] = band_ref[k]
        east_ref[EXT * HALO_SLABS :] = col_ref[...]
        west_ref[EXT * HALO_SLABS :] = jnp.zeros_like(col_ref)

    @pl.when(even_lon)
    def _():
        write(pa_ref, pb_ref)

    @pl.when(jnp.logical_not(even_lon))
    def _():
        write(pb_ref, pa_ref)


def gelu(x):
    return 0.5 * x * (1.0 + lax.erf(x * (0.5**0.5)))


def conv_kernel(
    band_ref, col_ref, ra_ref, rb_ref, keep_ref, w1_ref, b1_ref, w2_hbm, b2_ref,
    out_ref,
    w2_ref, w2_sem, west_col, joined, ext, hidden,
):
    load = pltpu.make_async_copy(w2_hbm, w2_ref, w2_sem)
    load.start()
    lat = lax.axis_index("lat")
    last = lax.axis_size("lat") - 1
    out_ch = b1_ref.shape[1]
    even_lon = lax.rem(lax.axis_index("lon"), 2) == 0
    halves = [slice(h * LANES, (h + 1) * LANES) for h in range(2)]

    def take(w_ref, e_ref):
        for k in range(HALO_SLABS):
            ext[k] = w_ref[EXT * k : EXT * (k + 1)]
            if k > 0:
                ext[HALO_SLABS + SLABS + k] = e_ref[EXT * k : EXT * (k + 1)]
        west_col[...] = w_ref[EXT * HALO_SLABS :].astype(F32)
        for h, at in enumerate(halves):
            joined[1, h] = e_ref[0:EXT, at].astype(F32)

    @pl.when(even_lon)
    def _():
        take(rb_ref, ra_ref)

    @pl.when(jnp.logical_not(even_lon))
    def _():
        take(ra_ref, rb_ref)

    for k in range(1, SLABS):
        ext[HALO_SLABS + k] = band_ref[k]
    firsts = pl.ds(0, EXT_R, stride=GROUP)
    for h, at in enumerate(halves):
        joined[0, h] = band_ref[0, :, at].astype(F32)
        joined[0, h, firsts, :] += west_col[0:EXT_R, at]
        joined[1, h, firsts, :] += col_ref[0:EXT_R, at].astype(F32)
        for side in range(2):
            ext[HALO_SLABS + SLABS * side, :, at] = resolved(joined[side, h]).astype(BF16)

    place = lax.broadcasted_iota(jnp.int32, (HID, 1), 0)
    inside = jnp.logical_and(
        jnp.logical_or(place >= 8 * GROUP, lat > 0),
        jnp.logical_or(place < HID - 8 * GROUP, lat < last),
    )

    def first(k, _):
        total = jnp.zeros((HID, out_ch), F32) + b1_ref[...]
        for a in range(3):
            for b in range(3):
                piece = ext[k + b, 4 * GROUP * a : 4 * GROUP * a + HID]
                total = total + jnp.dot(piece, w1_ref[a, b], preferred_element_type=F32)
        hidden[k] = jnp.where(inside, gelu(total), 0.0).astype(BF16)
        return 0

    lax.fori_loop(0, HID_SLABS, first, 0)
    load.wait()

    for k in range(SLABS):
        total = jnp.zeros((OWN, out_ch), F32) + b2_ref[...]
        for a in range(3):
            for b in range(3):
                piece = hidden[k + 2 * b, 8 * GROUP * a : 8 * GROUP * a + OWN]
                total = total + jnp.dot(piece, w2_ref[a, b], preferred_element_type=F32)
        kept = keep_ref[k]
        kept = jnp.concatenate([kept] * pl.cdiv(out_ch, LANES), axis=1)[:, :out_ch]
        value = (gelu(total) * kept).reshape(ROWS, GROUP, out_ch)
        out_ref[:, GROUP * k : GROUP * (k + 1), :] = value


def partners(axis, start, periodic):
    count = lax.axis_size(axis)
    route = []
    for i in range(start, count, 2):
        j = i + 1
        if j == count and not periodic:
            continue
        route += [(i, j % count), (j % count, i)]
    return route


def in_hbm(array):
    return pltpu.with_memory_space_constraint(array, pltpu.HBM)


def on_device(fields, land_sea, w_depth, b_depth, w_one, b_one, w_two, b_two):
    chans = fields.shape[2]
    out_ch = w_one.shape[3]
    vmem = pl.BlockSpec(memory_space=pltpu.VMEM)
    hbm = pl.BlockSpec(memory_space=pltpu.HBM)

    def shape(*dims, dtype=BF16):
        return jax.ShapeDtypeStruct(dims, dtype)

    lat_rows = SLABS * EDGE + 32
    lon_rows = HALO_SLABS * EXT + 64
    own, below, edge, keep, lat_a, lat_b = pl.pallas_call(
        down_kernel,
        out_shape=(
            shape(SLABS, OWN, chans),
            shape(COLS, chans),
            shape(ROWS + 16, chans),
            shape(SLABS, OWN, LANES, dtype=F32),
            shape(lat_rows, chans),
            shape(lat_rows, chans),
        ),
        in_specs=[hbm] * 4,
        out_specs=[vmem] * 6,
        scratch_shapes=[
            pltpu.VMEM((2, 2 * ROWS, 2 * COLS, LANES), F32),
            pltpu.VMEM((COLS, ROWS), jnp.int32),
            pltpu.VMEM(w_depth.shape, F32),
            pltpu.VMEM((1, chans), F32),
            pltpu.SemaphoreType.DMA((2, CHUNKS)),
            pltpu.SemaphoreType.DMA((3,)),
            pltpu.VMEM((ROWS * COLS, LANES), F32),
            pltpu.VMEM((SLABS, OWN, chans), F32),
            pltpu.VMEM((ROWS + 16, chans), F32),
        ],
        compiler_params=pltpu.CompilerParams(vmem_limit_bytes=16 << 20),
        name="down",
    )(in_hbm(fields), in_hbm(land_sea.T), in_hbm(w_depth), in_hbm(b_depth[None]))

    got_b = lax.ppermute(lat_b, "lat", partners("lat", 1, False))
    got_a = lax.ppermute(lat_a, "lat", partners("lat", 0, False))

    band, col, lon_a, lon_b = pl.pallas_call(
        band_kernel,
        out_shape=(
            shape(SLABS, EXT, chans),
            shape(64, chans),
            shape(lon_rows, chans),
            shape(lon_rows, chans),
        ),
        in_specs=[vmem] * 5,
        out_specs=[vmem] * 4,
        scratch_shapes=[
            pltpu.VMEM((lat_rows, chans), BF16),
            pltpu.VMEM((lat_rows, chans), BF16),
            pltpu.VMEM((2, SLABS, 16, chans), F32),
            pltpu.VMEM((64, chans), F32),
        ],
        compiler_params=pltpu.CompilerParams(vmem_limit_bytes=16 << 20),
        name="band",
    )(own, below, edge, got_a, got_b)

    got_b = lax.ppermute(lon_b, "lon", partners("lon", 1, True))
    got_a = lax.ppermute(lon_a, "lon", partners("lon", 0, True))

    return pl.pallas_call(
        conv_kernel,
        out_shape=shape(ROWS, COLS, out_ch, dtype=F32),
        in_specs=[vmem] * 7 + [hbm, vmem],
        out_specs=vmem,
        scratch_shapes=[
            pltpu.VMEM(w_two.shape, BF16),
            pltpu.SemaphoreType.DMA,
            pltpu.VMEM((64, chans), F32),
            pltpu.VMEM((2, 2, EXT, LANES), F32),
            pltpu.VMEM((2 * HALO_SLABS + SLABS, EXT, chans), BF16),
            pltpu.VMEM((HID_SLABS, HID, out_ch), BF16),
        ],
        compiler_params=pltpu.CompilerParams(vmem_limit_bytes=32 << 20),
        name="convolve",
    )(band, col, got_a, got_b, keep, w_one, b_one[None], in_hbm(w_two), b_two[None])


def solution(mesh):
    return jax.shard_map(
        on_device,
        mesh=mesh,
        in_specs=(P("lat", "lon", None), P("lat", "lon"), P(), P(), P(), P(), P(), P()),
        out_specs=P("lat", "lon", None),
        check_vma=False,
    )
```

```python
import jax
import jax.numpy as jnp
from jax import lax
from jax.experimental import pallas as pl
from jax.experimental.pallas import tpu as pltpu
from jax.sharding import PartitionSpec as P

ROWS = 32
COLS = 16
HALO = 12
GROUP = 4
SLABS = COLS // GROUP
HALO_SLABS = HALO // GROUP
OWN = ROWS * GROUP
EXT_R = ROWS + 2 * HALO
EXT = EXT_R * GROUP
HID = (ROWS + 16) * GROUP
SIDE = (COLS + 16) // GROUP // 2
EDGE = HALO * GROUP
LANES = 128
CHUNKS = 4
MASKED = 2.0**100
LIMIT = 2.0**90
F32 = jnp.float32
BF16 = jnp.bfloat16


def resolved(x):
    return jnp.where(x > LIMIT, 0.0, x)


def down_kernel(
    f_hbm, ls_hbm, wd_hbm, bd_hbm,
    own_ref, below_ref, edge_ref, keep_ref, pa_ref, pb_ref,
    f_ref, ls_ref, wd_ref, bd_ref, f_sem, sems, mask, patch, edge,
):
    lat = lax.axis_index("lat")
    last = lat == lax.axis_size("lat") - 1
    small = [
        pltpu.make_async_copy(src, dst, sems.at[k])
        for k, (src, dst) in enumerate(((ls_hbm, ls_ref), (wd_hbm, wd_ref), (bd_hbm, bd_ref)))
    ]
    for copy in small:
        copy.start()
    tall = 2 * ROWS // CHUNKS
    copies = {}
    for h in range(2):
        for k in range(CHUNKS):
            copies[h, k] = pltpu.make_async_copy(
                f_hbm.at[pl.ds(k * tall, tall), :, pl.ds(h * LANES, LANES)],
                f_ref.at[h, pl.ds(k * tall, tall)],
                f_sem.at[h, k],
            )
            copies[h, k].start()
    for copy in small:
        copy.wait()

    sea = ls_ref[...].astype(F32)
    for i in range(ROWS):
        mask[COLS * i : COLS * (i + 1)] = jnp.broadcast_to(sea[:, i : i + 1], (COLS, LANES))
    edge[...] = jnp.zeros_like(edge)

    first = lax.broadcasted_iota(jnp.int32, (COLS, LANES), 0) == 0
    holed = jnp.where(first, MASKED, 0.0)
    scale = jnp.where(last, 0.0, 1.0)
    for h in range(2):
        at = slice(h * LANES, (h + 1) * LANES)
        weight = [
            [jnp.broadcast_to(wd_ref[a, b : b + 1, at], (COLS, LANES)) for b in range(3)]
            for a in range(3)
        ]
        bias = jnp.broadcast_to(bd_ref[:, at], (COLS, LANES))
        for i in range(ROWS + 1):
            if i < ROWS and (2 * i) % tall == 0:
                copies[h, 2 * i // tall].wait()
            here, after = None, None
            for a in range(3):
                r = 2 * i - 1 + a
                if r < 0 or r >= 2 * ROWS:
                    continue
                even = f_ref[h, r, pl.ds(0, COLS, stride=2), :]
                odd = f_ref[h, r, pl.ds(1, COLS, stride=2), :]
                p = even * weight[a][1] + odd * weight[a][2]
                q = odd * weight[a][0]
                here = p if here is None else here + p
                after = q if after is None else after + q
            if i == ROWS:
                here, after = here * scale, after * scale
            else:
                here = here + bias
            moved = pltpu.roll(after, 1, 0)
            edge[i : i + 1, at] = moved[0:1]
            value = here + jnp.where(first, 0.0, moved)
            if i == ROWS:
                below_ref[:, at] = value.astype(BF16)
                continue
            kept = mask[COLS * i : COLS * (i + 1)]
            value = jnp.where(kept > 0.5, value, MASKED if i == 0 else holed)
            for q in range(SLABS):
                cells = slice(GROUP * i, GROUP * (i + 1))
                patch[q, cells, at] = value[GROUP * q : GROUP * (q + 1)]
                if h == 0:
                    keep_ref[q, cells] = kept[GROUP * q : GROUP * (q + 1)]

    own_ref[...] = patch[...].astype(BF16)
    edge_ref[...] = edge[...].astype(BF16)

    def write(south_ref, north_ref):
        for q in range(SLABS):
            south_ref[EDGE * q : EDGE * (q + 1)] = own_ref[q, OWN - EDGE : OWN]
            north_ref[EDGE * q : EDGE * (q + 1)] = own_ref[q, 0:EDGE]
        base = EDGE * SLABS
        south_ref[base : base + 16] = below_ref[...]
        south_ref[base + 16 : base + 32] = edge[ROWS - HALO : ROWS - HALO + 16].astype(BF16)
        north_ref[base : base + 16] = edge[0:16].astype(BF16)
        north_ref[base + 16 : base + 32] = jnp.zeros((16, 2 * LANES), BF16)

    even = lax.rem(lat, 2) == 0

    @pl.when(even)
    def _():
        write(pa_ref, pb_ref)

    @pl.when(jnp.logical_not(even))
    def _():
        write(pb_ref, pa_ref)


def band_kernel(
    own_ref, below_ref, edge_ref, rb_ref, ra_ref,
    band_ref, col_ref, pa_ref, pb_ref,
    north, south, tile, col,
):
    even_lat = lax.rem(lax.axis_index("lat"), 2) == 0
    even_lon = lax.rem(lax.axis_index("lon"), 2) == 0

    @pl.when(even_lat)
    def _():
        south[...] = ra_ref[...]
        north[...] = rb_ref[...]

    @pl.when(jnp.logical_not(even_lat))
    def _():
        north[...] = ra_ref[...]
        south[...] = rb_ref[...]

    base = EDGE * SLABS
    col[HALO : HALO + ROWS + 16] = edge_ref[...].astype(F32)
    n_edge = north[base + 16 : base + 32].astype(F32)
    s_edge = south[base : base + 16].astype(F32)
    col[0:HALO] = n_edge[0:HALO]
    col[HALO : HALO + 1] += n_edge[HALO : HALO + 1]
    col[HALO + ROWS : HALO + ROWS + 1] += s_edge[0:1]
    col[HALO + ROWS + 1 : EXT_R] = s_edge[1:HALO]
    col_ref[...] = col[...].astype(BF16)

    above = north[base : base + 16].astype(F32)
    below = below_ref[...].astype(F32)
    for q in range(SLABS):
        cells = slice(GROUP * q, GROUP * (q + 1))
        tile[0, q] = own_ref[q, 0:16].astype(F32)
        tile[1, q] = south[EDGE * q : EDGE * q + 16].astype(F32)
        tile[0, q, 0:GROUP] += above[cells]
        tile[1, q, 0:GROUP] += below[cells]
        top, bottom = tile[0, q], tile[1, q]
        if q > 0:
            top, bottom = resolved(top), resolved(bottom)
        band_ref[q, 0:EDGE] = north[EDGE * q : EDGE * (q + 1)]
        band_ref[q, EDGE : EDGE + 16] = top.astype(BF16)
        band_ref[q, EDGE + 16 : EDGE + OWN] = own_ref[q, 16:OWN]
        band_ref[q, EDGE + OWN : EDGE + OWN + 16] = bottom.astype(BF16)
        band_ref[q, EDGE + OWN + 16 : EXT] = south[EDGE * q + 16 : EDGE * (q + 1)]

    def write(east_ref, west_ref):
        for k in range(HALO_SLABS):
            east_ref[EXT * k : EXT * (k + 1)] = band_ref[SLABS - HALO_SLABS + k]
            west_ref[EXT * k : EXT * (k + 1)] = band_ref[k]
        east_ref[EXT * HALO_SLABS :] = col_ref[...]
        west_ref[EXT * HALO_SLABS :] = jnp.zeros_like(col_ref)

    @pl.when(even_lon)
    def _():
        write(pa_ref, pb_ref)

    @pl.when(jnp.logical_not(even_lon))
    def _():
        write(pb_ref, pa_ref)


def gelu(x):
    return 0.5 * x * (1.0 + lax.erf(x * (0.5**0.5)))


def half_sums(
    side_west, band_ref, col_ref, far_ref, w1_ref, b1_ref, w2_ref, load, sums,
    west_col, joined, ext, hidden,
):
    lat = lax.axis_index("lat")
    last = lax.axis_size("lat") - 1
    out_ch = b1_ref.shape[1]
    side_east = jnp.logical_not(side_west)
    halves = [slice(h * LANES, (h + 1) * LANES) for h in range(2)]
    firsts = pl.ds(0, EXT_R, stride=GROUP)

    @pl.when(side_west)
    def _():
        west_col[...] = far_ref[EXT * HALO_SLABS :].astype(F32)
        for k in range(HALO_SLABS):
            ext[k] = far_ref[EXT * k : EXT * (k + 1)]
        for k in range(1, HALO_SLABS):
            ext[HALO_SLABS + k] = band_ref[k]
        for h, at in enumerate(halves):
            joined[h] = band_ref[0, :, at].astype(F32)

    @pl.when(side_east)
    def _():
        west_col[...] = col_ref[...].astype(F32)
        for k in range(1, HALO_SLABS):
            ext[HALO_SLABS + k] = far_ref[EXT * k : EXT * (k + 1)]
        for k in range(HALO_SLABS):
            ext[k] = band_ref[k + 1]
        for h, at in enumerate(halves):
            joined[h] = far_ref[0:EXT, at].astype(F32)

    for h, at in enumerate(halves):
        joined[h, firsts, :] += west_col[0:EXT_R, at]
        ext[HALO_SLABS, :, at] = resolved(joined[h]).astype(BF16)

    place = lax.broadcasted_iota(jnp.int32, (HID, 1), 0)
    inside = jnp.logical_and(
        jnp.logical_or(place >= 8 * GROUP, lat > 0),
        jnp.logical_or(place < HID - 8 * GROUP, lat < last),
    )
    for k in range(SIDE):
        total = jnp.zeros((HID, out_ch), F32) + b1_ref[...]
        for a in range(3):
            for b in range(3):
                piece = ext[k + b, 4 * GROUP * a : 4 * GROUP * a + HID]
                total = total + jnp.dot(piece, w1_ref[a, b], preferred_element_type=F32)
        hidden[k] = jnp.where(inside, gelu(total), 0.0).astype(BF16)
    load.wait()

    def second(first_slab):
        for k in range(SLABS):
            total = sums[k]
            for b in range(3):
                slab = k + 2 * b - first_slab
                if slab < 0 or slab >= SIDE:
                    continue
                for a in range(3):
                    piece = hidden[slab, 8 * GROUP * a : 8 * GROUP * a + OWN]
                    total = total + jnp.dot(piece, w2_ref[a, b], preferred_element_type=F32)
            sums[k] = total

    @pl.when(side_west)
    def _():
        second(0)

    @pl.when(side_east)
    def _():
        second(SIDE)


def near_kernel(
    band_ref, col_ref, far_ref, w1_ref, b1_ref, w2_hbm, b2_ref,
    sums_ref,
    w2_ref, w2_sem, west_col, joined, ext, hidden,
):
    load = pltpu.make_async_copy(w2_hbm, w2_ref, w2_sem)
    load.start()
    sums_ref[...] = jnp.broadcast_to(b2_ref[...], sums_ref.shape)
    odd = lax.rem(lax.axis_index("lon"), 2) == 1
    half_sums(
        odd, band_ref, col_ref, far_ref, w1_ref, b1_ref, w2_ref, load, sums_ref,
        west_col, joined, ext, hidden,
    )


def far_kernel(
    band_ref, col_ref, far_ref, w1_ref, b1_ref, w2_hbm, near_ref, keep_ref,
    out_ref,
    w2_ref, w2_sem, west_col, joined, ext, hidden, sums,
):
    load = pltpu.make_async_copy(w2_hbm, w2_ref, w2_sem)
    load.start()
    out_ch = b1_ref.shape[1]
    sums[...] = near_ref[...]
    even = lax.rem(lax.axis_index("lon"), 2) == 0
    half_sums(
        even, band_ref, col_ref, far_ref, w1_ref, b1_ref, w2_ref, load, sums,
        west_col, joined, ext, hidden,
    )
    for k in range(SLABS):
        kept = keep_ref[k]
        kept = jnp.concatenate([kept] * pl.cdiv(out_ch, LANES), axis=1)[:, :out_ch]
        value = (gelu(sums[k]) * kept).reshape(ROWS, GROUP, out_ch)
        out_ref[:, GROUP * k : GROUP * (k + 1), :] = value


def partners(axis, start, periodic):
    count = lax.axis_size(axis)
    route = []
    for i in range(start, count, 2):
        j = i + 1
        if j == count and not periodic:
            continue
        route += [(i, j % count), (j % count, i)]
    return route


def in_hbm(array):
    return pltpu.with_memory_space_constraint(array, pltpu.HBM)


def on_device(fields, land_sea, w_depth, b_depth, w_one, b_one, w_two, b_two):
    chans = fields.shape[2]
    out_ch = w_one.shape[3]
    vmem = pl.BlockSpec(memory_space=pltpu.VMEM)
    hbm = pl.BlockSpec(memory_space=pltpu.HBM)

    def shape(*dims, dtype=BF16):
        return jax.ShapeDtypeStruct(dims, dtype)

    lat_rows = SLABS * EDGE + 32
    lon_rows = HALO_SLABS * EXT + 64
    own, below, edge, keep, lat_a, lat_b = pl.pallas_call(
        down_kernel,
        out_shape=(
            shape(SLABS, OWN, chans),
            shape(COLS, chans),
            shape(ROWS + 16, chans),
            shape(SLABS, OWN, LANES, dtype=F32),
            shape(lat_rows, chans),
            shape(lat_rows, chans),
        ),
        in_specs=[hbm] * 4,
        out_specs=[vmem] * 6,
        scratch_shapes=[
            pltpu.VMEM((2, 2 * ROWS, 2 * COLS, LANES), F32),
            pltpu.VMEM((COLS, ROWS), jnp.int32),
            pltpu.VMEM(w_depth.shape, F32),
            pltpu.VMEM((1, chans), F32),
            pltpu.SemaphoreType.DMA((2, CHUNKS)),
            pltpu.SemaphoreType.DMA((3,)),
            pltpu.VMEM((ROWS * COLS, LANES), F32),
            pltpu.VMEM((SLABS, OWN, chans), F32),
            pltpu.VMEM((ROWS + 16, chans), F32),
        ],
        compiler_params=pltpu.CompilerParams(vmem_limit_bytes=10 << 20),
        name="down",
    )(in_hbm(fields), in_hbm(land_sea.T), in_hbm(w_depth), in_hbm(b_depth[None]))

    got_b = lax.ppermute(lat_b, "lat", partners("lat", 1, False))
    got_a = lax.ppermute(lat_a, "lat", partners("lat", 0, False))

    band, col, lon_a, lon_b = pl.pallas_call(
        band_kernel,
        out_shape=(
            shape(SLABS, EXT, chans),
            shape(64, chans),
            shape(lon_rows, chans),
            shape(lon_rows, chans),
        ),
        in_specs=[vmem] * 5,
        out_specs=[vmem] * 4,
        scratch_shapes=[
            pltpu.VMEM((lat_rows, chans), BF16),
            pltpu.VMEM((lat_rows, chans), BF16),
            pltpu.VMEM((2, SLABS, 16, chans), F32),
            pltpu.VMEM((64, chans), F32),
        ],
        compiler_params=pltpu.CompilerParams(vmem_limit_bytes=10 << 20),
        name="band",
    )(own, below, edge, got_b, got_a)

    got_b = lax.ppermute(lon_b, "lon", partners("lon", 1, True))
    got_a = lax.ppermute(lon_a, "lon", partners("lon", 0, True))

    scratch = [
        pltpu.VMEM(w_two.shape, BF16),
        pltpu.SemaphoreType.DMA,
        pltpu.VMEM((64, chans), F32),
        pltpu.VMEM((2, EXT, LANES), F32),
        pltpu.VMEM((2 * HALO_SLABS, EXT, chans), BF16),
        pltpu.VMEM((SIDE, HID, out_ch), BF16),
    ]
    w_two, b_one = in_hbm(w_two), b_one[None]
    flops = 2 * SIDE * HID * 9 * chans * out_ch + 2 * 6 * OWN * 3 * out_ch * out_ch
    cost = pl.CostEstimate(flops=flops, bytes_accessed=4 << 20, transcendentals=SIDE * HID * out_ch)
    near = pl.pallas_call(
        near_kernel,
        out_shape=shape(SLABS, OWN, out_ch, dtype=F32),
        in_specs=[vmem] * 5 + [hbm, vmem],
        out_specs=vmem,
        scratch_shapes=scratch,
        compiler_params=pltpu.CompilerParams(vmem_limit_bytes=14 << 20),
        cost_estimate=cost,
        name="near_half",
    )(band, col, got_a, w_one, b_one, w_two, b_two[None])

    return pl.pallas_call(
        far_kernel,
        out_shape=shape(ROWS, COLS, out_ch, dtype=F32),
        in_specs=[vmem] * 5 + [hbm, vmem, vmem],
        out_specs=vmem,
        scratch_shapes=scratch + [pltpu.VMEM((SLABS, OWN, out_ch), F32)],
        compiler_params=pltpu.CompilerParams(vmem_limit_bytes=14 << 20),
        cost_estimate=cost,
        name="far_half",
    )(band, col, got_b, w_one, b_one, w_two, near, keep)


def solution(mesh):
    return jax.shard_map(
        on_device,
        mesh=mesh,
        in_specs=(P("lat", "lon", None), P("lat", "lon"), P(), P(), P(), P(), P(), P()),
        out_specs=P("lat", "lon", None),
        check_vma=False,
    )
```

```python
import jax
import jax.numpy as jnp
from jax import lax
from jax.experimental import pallas as pl
from jax.experimental.layout import Layout, with_layout_constraint
from jax.experimental.pallas import tpu as pltpu
from jax.sharding import PartitionSpec as P

ROWS = 32
COLS = 16
HALO = 12
GROUP = 4
SLABS = COLS // GROUP
HALO_SLABS = HALO // GROUP
OWN = ROWS * GROUP
EXT_R = ROWS + 2 * HALO
EXT = EXT_R * GROUP
HID = (ROWS + 16) * GROUP
SIDE = (COLS + 16) // GROUP // 2
EDGE = HALO * GROUP
LANES = 128
CHUNKS = 4
MASKED = 2.0**100
LIMIT = 2.0**90
F32 = jnp.float32
BF16 = jnp.bfloat16


def resolved(x):
    return jnp.where(x > LIMIT, 0.0, x)


def down_kernel(
    f_hbm, ls_hbm, wd_hbm, bd_hbm,
    own_ref, below_ref, edge_ref, keep_ref, south_ref, pa_ref, north_ref,
    f_ref, ls_ref, wd_ref, bd_ref, f_sem, sems, mask, patch, edge,
):
    lat = lax.axis_index("lat")
    last = lat == lax.axis_size("lat") - 1
    small = [
        pltpu.make_async_copy(src, dst, sems.at[k])
        for k, (src, dst) in enumerate(((ls_hbm, ls_ref), (wd_hbm, wd_ref), (bd_hbm, bd_ref)))
    ]
    for copy in small:
        copy.start()
    tall = 2 * ROWS // CHUNKS
    copies = {}
    for h in range(2):
        for k in range(CHUNKS):
            copies[h, k] = pltpu.make_async_copy(
                f_hbm.at[pl.ds(k * tall, tall), :, pl.ds(h * LANES, LANES)],
                f_ref.at[h, pl.ds(k * tall, tall)],
                f_sem.at[h, k],
            )
            copies[h, k].start()
    for copy in small:
        copy.wait()

    sea = ls_ref[...].astype(F32)
    for i in range(ROWS):
        mask[COLS * i : COLS * (i + 1)] = jnp.broadcast_to(sea[:, i : i + 1], (COLS, LANES))
    edge[...] = jnp.zeros_like(edge)

    first = lax.broadcasted_iota(jnp.int32, (COLS, LANES), 0) == 0
    holed = jnp.where(first, MASKED, 0.0)
    scale = jnp.where(last, 0.0, 1.0)
    for h in range(2):
        at = slice(h * LANES, (h + 1) * LANES)
        weight = [
            [jnp.broadcast_to(wd_ref[a, b : b + 1, at], (COLS, LANES)) for b in range(3)]
            for a in range(3)
        ]
        bias = jnp.broadcast_to(bd_ref[:, at], (COLS, LANES))
        for i in range(ROWS + 1):
            if i < ROWS and (2 * i) % tall == 0:
                copies[h, 2 * i // tall].wait()
            here, after = None, None
            for a in range(3):
                r = 2 * i - 1 + a
                if r < 0 or r >= 2 * ROWS:
                    continue
                even = f_ref[h, r, pl.ds(0, COLS, stride=2), :]
                odd = f_ref[h, r, pl.ds(1, COLS, stride=2), :]
                p = even * weight[a][1] + odd * weight[a][2]
                q = odd * weight[a][0]
                here = p if here is None else here + p
                after = q if after is None else after + q
            if i == ROWS:
                here, after = here * scale, after * scale
            else:
                here = here + bias
            moved = pltpu.roll(after, 1, 0)
            edge[i : i + 1, at] = moved[0:1]
            value = here + jnp.where(first, 0.0, moved)
            if i == ROWS:
                below_ref[:, at] = value.astype(BF16)
                continue
            kept = mask[COLS * i : COLS * (i + 1)]
            value = jnp.where(kept > 0.5, value, MASKED if i == 0 else holed)
            for q in range(SLABS):
                cells = slice(GROUP * i, GROUP * (i + 1))
                patch[q, cells, at] = value[GROUP * q : GROUP * (q + 1)]
                if h == 0:
                    keep_ref[q, cells] = kept[GROUP * q : GROUP * (q + 1)]

    own_ref[...] = patch[...].astype(BF16)
    edge_ref[...] = edge[...].astype(BF16)

    for q in range(SLABS):
        south_ref[EDGE * q : EDGE * (q + 1)] = own_ref[q, OWN - EDGE : OWN]
        north_ref[EDGE * q : EDGE * (q + 1)] = own_ref[q, 0:EDGE]
    base = EDGE * SLABS
    south_ref[base : base + 16] = below_ref[...]
    south_ref[base + 16 : base + 32] = edge[ROWS - HALO : ROWS - HALO + 16].astype(BF16)
    north_ref[base : base + 16] = edge[0:16].astype(BF16)
    north_ref[base + 16 : base + 32] = jnp.zeros((16, 2 * LANES), BF16)

    even = lax.rem(lat, 2) == 0

    @pl.when(even)
    def _():
        pa_ref[...] = south_ref[...]

    @pl.when(jnp.logical_not(even))
    def _():
        pa_ref[...] = north_ref[...]


def band_kernel(
    own_ref, below_ref, edge_ref, down_ref, ra_ref, up_ref,
    band_ref, col_ref, pa_ref, pb_ref,
    north, south, tile, col,
):
    even_lat = lax.rem(lax.axis_index("lat"), 2) == 0
    even_lon = lax.rem(lax.axis_index("lon"), 2) == 0

    @pl.when(even_lat)
    def _():
        south[...] = ra_ref[...]
        north[...] = down_ref[...]

    @pl.when(jnp.logical_not(even_lat))
    def _():
        north[...] = ra_ref[...]
        south[...] = up_ref[...]

    base = EDGE * SLABS
    col[HALO : HALO + ROWS + 16] = edge_ref[...].astype(F32)
    n_edge = north[base + 16 : base + 32].astype(F32)
    s_edge = south[base : base + 16].astype(F32)
    col[0:HALO] = n_edge[0:HALO]
    col[HALO : HALO + 1] += n_edge[HALO : HALO + 1]
    col[HALO + ROWS : HALO + ROWS + 1] += s_edge[0:1]
    col[HALO + ROWS + 1 : EXT_R] = s_edge[1:HALO]
    col_ref[...] = col[...].astype(BF16)

    above = north[base : base + 16].astype(F32)
    below = below_ref[...].astype(F32)
    for q in range(SLABS):
        cells = slice(GROUP * q, GROUP * (q + 1))
        tile[0, q] = own_ref[q, 0:16].astype(F32)
        tile[1, q] = south[EDGE * q : EDGE * q + 16].astype(F32)
        tile[0, q, 0:GROUP] += above[cells]
        tile[1, q, 0:GROUP] += below[cells]
        top, bottom = tile[0, q], tile[1, q]
        if q > 0:
            top, bottom = resolved(top), resolved(bottom)
        band_ref[q, 0:EDGE] = north[EDGE * q : EDGE * (q + 1)]
        band_ref[q, EDGE : EDGE + 16] = top.astype(BF16)
        band_ref[q, EDGE + 16 : EDGE + OWN] = own_ref[q, 16:OWN]
        band_ref[q, EDGE + OWN : EDGE + OWN + 16] = bottom.astype(BF16)
        band_ref[q, EDGE + OWN + 16 : EXT] = south[EDGE * q + 16 : EDGE * (q + 1)]

    def write(east_ref, west_ref):
        for k in range(HALO_SLABS):
            east_ref[EXT * k : EXT * (k + 1)] = band_ref[SLABS - HALO_SLABS + k]
            west_ref[EXT * k : EXT * (k + 1)] = band_ref[k]
        east_ref[EXT * HALO_SLABS :] = col_ref[...]
        west_ref[EXT * HALO_SLABS :] = jnp.zeros_like(col_ref)

    @pl.when(even_lon)
    def _():
        write(pa_ref, pb_ref)

    @pl.when(jnp.logical_not(even_lon))
    def _():
        write(pb_ref, pa_ref)


def gelu(x):
    return 0.5 * x * (1.0 + lax.erf(x * (0.5**0.5)))


def half_sums(
    side_west, band_ref, col_ref, from_west, from_east, w1_ref, b1_ref, w2_ref, load, sums,
    west_col, joined, ext, hidden,
):
    lat = lax.axis_index("lat")
    last = lax.axis_size("lat") - 1
    out_ch = b1_ref.shape[1]
    side_east = jnp.logical_not(side_west)
    halves = [slice(h * LANES, (h + 1) * LANES) for h in range(2)]
    firsts = pl.ds(0, EXT_R, stride=GROUP)

    @pl.when(side_west)
    def _():
        west_col[...] = from_west[EXT * HALO_SLABS :].astype(F32)
        for k in range(HALO_SLABS):
            ext[k] = from_west[EXT * k : EXT * (k + 1)]
        for k in range(1, HALO_SLABS):
            ext[HALO_SLABS + k] = band_ref[k]
        for h, at in enumerate(halves):
            joined[h] = band_ref[0, :, at].astype(F32)

    @pl.when(side_east)
    def _():
        west_col[...] = col_ref[...].astype(F32)
        for k in range(1, HALO_SLABS):
            ext[HALO_SLABS + k] = from_east[EXT * k : EXT * (k + 1)]
        for k in range(HALO_SLABS):
            ext[k] = band_ref[k + 1]
        for h, at in enumerate(halves):
            joined[h] = from_east[0:EXT, at].astype(F32)

    for h, at in enumerate(halves):
        joined[h, firsts, :] += west_col[0:EXT_R, at]
        ext[HALO_SLABS, :, at] = resolved(joined[h]).astype(BF16)

    place = lax.broadcasted_iota(jnp.int32, (HID, 1), 0)
    inside = jnp.logical_and(
        jnp.logical_or(place >= 8 * GROUP, lat > 0),
        jnp.logical_or(place < HID - 8 * GROUP, lat < last),
    )
    for k in range(SIDE):
        total = jnp.zeros((HID, out_ch), F32) + b1_ref[...]
        for a in range(3):
            for b in range(3):
                piece = ext[k + b, 4 * GROUP * a : 4 * GROUP * a + HID]
                total = total + jnp.dot(piece, w1_ref[a, b], preferred_element_type=F32)
        hidden[k] = jnp.where(inside, gelu(total), 0.0).astype(BF16)
    load.wait()

    def second(first_slab):
        for k in range(SLABS):
            total = sums[k]
            for b in range(3):
                slab = k + 2 * b - first_slab
                if slab < 0 or slab >= SIDE:
                    continue
                for a in range(3):
                    piece = hidden[slab, 8 * GROUP * a : 8 * GROUP * a + OWN]
                    total = total + jnp.dot(piece, w2_ref[a, b], preferred_element_type=F32)
            sums[k] = total

    @pl.when(side_west)
    def _():
        second(0)

    @pl.when(side_east)
    def _():
        second(SIDE)


def near_kernel(
    band_ref, col_ref, both_ref, w1_ref, b1_ref, w2_hbm, b2_ref,
    sums_ref,
    w2_ref, w2_sem, west_col, joined, ext, hidden,
):
    load = pltpu.make_async_copy(w2_hbm, w2_ref, w2_sem)
    load.start()
    sums_ref[...] = jnp.broadcast_to(b2_ref[...], sums_ref.shape)
    odd = lax.rem(lax.axis_index("lon"), 2) == 1
    half_sums(
        odd, band_ref, col_ref, both_ref.at[0], both_ref.at[1], w1_ref, b1_ref, w2_ref, load, sums_ref,
        west_col, joined, ext, hidden,
    )


def far_kernel(
    band_ref, col_ref, far_ref, w1_ref, b1_ref, w2_hbm, near_ref, keep_ref,
    out_ref,
    w2_ref, w2_sem, west_col, joined, ext, hidden, sums,
):
    load = pltpu.make_async_copy(w2_hbm, w2_ref, w2_sem)
    load.start()
    out_ch = b1_ref.shape[1]
    sums[...] = near_ref[...]
    even = lax.rem(lax.axis_index("lon"), 2) == 0
    half_sums(
        even, band_ref, col_ref, far_ref, far_ref, w1_ref, b1_ref, w2_ref, load, sums,
        west_col, joined, ext, hidden,
    )
    for k in range(SLABS):
        kept = keep_ref[k]
        kept = jnp.concatenate([kept] * pl.cdiv(out_ch, LANES), axis=1)[:, :out_ch]
        value = (gelu(sums[k]) * kept).reshape(ROWS, GROUP, out_ch)
        out_ref[:, GROUP * k : GROUP * (k + 1), :] = value


def partners(axis, start, periodic):
    count = lax.axis_size(axis)
    route = []
    for i in range(start, count, 2):
        j = i + 1
        if j == count and not periodic:
            continue
        route += [(i, j % count), (j % count, i)]
    return route


def in_hbm(array):
    return pltpu.with_memory_space_constraint(array, pltpu.HBM)


def on_device(fields, land_sea, w_depth, b_depth, w_one, b_one, w_two, b_two):
    chans = fields.shape[2]
    out_ch = w_one.shape[3]
    vmem = pl.BlockSpec(memory_space=pltpu.VMEM)
    hbm = pl.BlockSpec(memory_space=pltpu.HBM)

    def shape(*dims, dtype=BF16):
        return jax.ShapeDtypeStruct(dims, dtype)

    lat_rows = SLABS * EDGE + 32
    lon_rows = HALO_SLABS * EXT + 64
    own, below, edge, keep, to_south, to_partner, to_north = pl.pallas_call(
        down_kernel,
        out_shape=(
            shape(SLABS, OWN, chans),
            shape(COLS, chans),
            shape(ROWS + 16, chans),
            shape(SLABS, OWN, LANES, dtype=F32),
            shape(lat_rows, chans),
            shape(lat_rows, chans),
            shape(lat_rows, chans),
        ),
        in_specs=[hbm] * 4,
        out_specs=[vmem] * 7,
        scratch_shapes=[
            pltpu.VMEM((2, 2 * ROWS, 2 * COLS, LANES), F32),
            pltpu.VMEM((COLS, ROWS), jnp.int32),
            pltpu.VMEM(w_depth.shape, F32),
            pltpu.VMEM((1, chans), F32),
            pltpu.SemaphoreType.DMA((2, CHUNKS)),
            pltpu.SemaphoreType.DMA((3,)),
            pltpu.VMEM((ROWS * COLS, LANES), F32),
            pltpu.VMEM((SLABS, OWN, chans), F32),
            pltpu.VMEM((ROWS + 16, chans), F32),
        ],
        compiler_params=pltpu.CompilerParams(vmem_limit_bytes=10 << 20),
        name="down",
    )(in_hbm(fields), in_hbm(land_sea.T), in_hbm(w_depth), in_hbm(b_depth[None]))

    swaps = partners("lat", 1, False)
    got_down = lax.ppermute(to_south, "lat", [(i, j) for i, j in swaps if i < j])
    got_a = lax.ppermute(to_partner, "lat", partners("lat", 0, False))
    got_up = lax.ppermute(to_north, "lat", [(i, j) for i, j in swaps if i > j])

    w_one = with_layout_constraint(w_one, Layout((0, 1, 2, 3)))
    got_down, w_one = lax.optimization_barrier((got_down, w_one))

    band, col, lon_a, lon_b = pl.pallas_call(
        band_kernel,
        out_shape=(
            shape(SLABS, EXT, chans),
            shape(64, chans),
            shape(lon_rows, chans),
            shape(lon_rows, chans),
        ),
        in_specs=[vmem] * 6,
        out_specs=[vmem] * 4,
        scratch_shapes=[
            pltpu.VMEM((lat_rows, chans), BF16),
            pltpu.VMEM((lat_rows, chans), BF16),
            pltpu.VMEM((2, SLABS, 16, chans), F32),
            pltpu.VMEM((64, chans), F32),
        ],
        compiler_params=pltpu.CompilerParams(vmem_limit_bytes=10 << 20),
        name="band",
    )(own, below, edge, got_down, got_a, got_up)

    got_b = lax.ppermute(lon_b, "lon", partners("lon", 1, True))
    count = lax.axis_size("lon")
    chips = [[i, i + 1] for i in range(0, count, 2)]
    both = lax.all_gather(lon_a, "lon", axis_index_groups=chips)

    scratch = [
        pltpu.VMEM(w_two.shape, BF16),
        pltpu.SemaphoreType.DMA,
        pltpu.VMEM((64, chans), F32),
        pltpu.VMEM((2, EXT, LANES), F32),
        pltpu.VMEM((2 * HALO_SLABS, EXT, chans), BF16),
        pltpu.VMEM((SIDE, HID, out_ch), BF16),
    ]
    w_two, b_one = in_hbm(w_two), b_one[None]
    flops = 2 * SIDE * HID * 9 * chans * out_ch + 2 * 6 * OWN * 3 * out_ch * out_ch
    cost = pl.CostEstimate(flops=flops, bytes_accessed=4 << 20, transcendentals=SIDE * HID * out_ch)
    near = pl.pallas_call(
        near_kernel,
        out_shape=shape(SLABS, OWN, out_ch, dtype=F32),
        in_specs=[vmem] * 5 + [hbm, vmem],
        out_specs=vmem,
        scratch_shapes=scratch,
        compiler_params=pltpu.CompilerParams(vmem_limit_bytes=14 << 20),
        cost_estimate=cost,
        name="near_half",
    )(band, col, both, w_one, b_one, w_two, b_two[None])

    return pl.pallas_call(
        far_kernel,
        out_shape=shape(ROWS, COLS, out_ch, dtype=F32),
        in_specs=[vmem] * 5 + [hbm, vmem, vmem],
        out_specs=vmem,
        scratch_shapes=scratch + [pltpu.VMEM((SLABS, OWN, out_ch), F32)],
        compiler_params=pltpu.CompilerParams(vmem_limit_bytes=14 << 20),
        cost_estimate=cost,
        name="far_half",
    )(band, col, got_b, w_one, b_one, w_two, near, keep)


def solution(mesh):
    return jax.shard_map(
        on_device,
        mesh=mesh,
        in_specs=(P("lat", "lon", None), P("lat", "lon"), P(), P(), P(), P(), P(), P()),
        out_specs=P("lat", "lon", None),
        check_vma=False,
    )
```

```python
import jax
import jax.numpy as jnp
from jax import lax
from jax.experimental import pallas as pl
from jax.experimental.layout import Layout, with_layout_constraint
from jax.experimental.pallas import tpu as pltpu
from jax.sharding import PartitionSpec as P

ROWS = 32
COLS = 16
HALO = 12
GROUP = 4
SLABS = COLS // GROUP
HALO_SLABS = HALO // GROUP
OWN = ROWS * GROUP
EXT_R = ROWS + 2 * HALO
EXT = EXT_R * GROUP
HID = (ROWS + 16) * GROUP
SIDE = (COLS + 16) // GROUP // 2
EDGE = HALO * GROUP
LANES = 128
MAIN = 256
PAD = 64
CHUNKS = 4
MASKED = 2.0**100
LIMIT = 2.0**90
F32 = jnp.float32
BF16 = jnp.bfloat16


def resolved(x):
    return jnp.where(x > LIMIT, 0.0, x)


def down_kernel(
    f_hbm, ls_hbm, wd_hbm, bd_hbm,
    own_ref, below_ref, edge_ref, keep_ref, south_ref, pa_ref, north_ref,
    f_ref, ls_ref, wd_ref, bd_ref, f_sem, sems, mask, patch, edge,
):
    lat = lax.axis_index("lat")
    last = lat == lax.axis_size("lat") - 1
    small = [
        pltpu.make_async_copy(src, dst, sems.at[k])
        for k, (src, dst) in enumerate(((ls_hbm, ls_ref), (wd_hbm, wd_ref), (bd_hbm, bd_ref)))
    ]
    for copy in small:
        copy.start()
    tall = 2 * ROWS // CHUNKS
    copies = {}
    for h in range(2):
        for k in range(CHUNKS):
            copies[h, k] = pltpu.make_async_copy(
                f_hbm.at[pl.ds(k * tall, tall), :, pl.ds(h * LANES, LANES)],
                f_ref.at[h, pl.ds(k * tall, tall)],
                f_sem.at[h, k],
            )
            copies[h, k].start()
    for copy in small:
        copy.wait()

    sea = ls_ref[...].astype(F32)
    for i in range(ROWS):
        mask[COLS * i : COLS * (i + 1)] = jnp.broadcast_to(sea[:, i : i + 1], (COLS, LANES))
    edge[...] = jnp.zeros_like(edge)

    first = lax.broadcasted_iota(jnp.int32, (COLS, LANES), 0) == 0
    holed = jnp.where(first, MASKED, 0.0)
    scale = jnp.where(last, 0.0, 1.0)
    for h in range(2):
        at = slice(h * LANES, (h + 1) * LANES)
        weight = [
            [jnp.broadcast_to(wd_ref[a, b : b + 1, at], (COLS, LANES)) for b in range(3)]
            for a in range(3)
        ]
        bias = jnp.broadcast_to(bd_ref[:, at], (COLS, LANES))
        for i in range(ROWS + 1):
            if i < ROWS and (2 * i) % tall == 0:
                copies[h, 2 * i // tall].wait()
            here, after = None, None
            for a in range(3):
                r = 2 * i - 1 + a
                if r < 0 or r >= 2 * ROWS:
                    continue
                even = f_ref[h, r, pl.ds(0, COLS, stride=2), :]
                odd = f_ref[h, r, pl.ds(1, COLS, stride=2), :]
                p = even * weight[a][1] + odd * weight[a][2]
                q = odd * weight[a][0]
                here = p if here is None else here + p
                after = q if after is None else after + q
            if i == ROWS:
                here, after = here * scale, after * scale
            else:
                here = here + bias
            moved = pltpu.roll(after, 1, 0)
            edge[i : i + 1, at] = moved[0:1]
            value = here + jnp.where(first, 0.0, moved)
            if i == ROWS:
                below_ref[:, at] = value.astype(BF16)
                continue
            kept = mask[COLS * i : COLS * (i + 1)]
            value = jnp.where(kept > 0.5, value, MASKED if i == 0 else holed)
            for q in range(SLABS):
                cells = slice(GROUP * i, GROUP * (i + 1))
                patch[q, cells, at] = value[GROUP * q : GROUP * (q + 1)]
                if h == 0:
                    keep_ref[q, cells] = kept[GROUP * q : GROUP * (q + 1)]

    own_ref[...] = patch[...].astype(BF16)
    edge_ref[...] = edge[...].astype(BF16)

    for q in range(SLABS):
        south_ref[EDGE * q : EDGE * (q + 1)] = own_ref[q, OWN - EDGE : OWN]
        north_ref[EDGE * q : EDGE * (q + 1)] = own_ref[q, 0:EDGE]
    base = EDGE * SLABS
    south_ref[base : base + 16] = below_ref[...]
    south_ref[base + 16 : base + 32] = edge[ROWS - HALO : ROWS - HALO + 16].astype(BF16)
    north_ref[base : base + 16] = edge[0:16].astype(BF16)
    north_ref[base + 16 : base + 32] = jnp.zeros((16, 2 * LANES), BF16)

    even = lax.rem(lat, 2) == 0

    @pl.when(even)
    def _():
        pa_ref[...] = south_ref[...]

    @pl.when(jnp.logical_not(even))
    def _():
        pa_ref[...] = north_ref[...]


def band_kernel(
    own_ref, below_ref, edge_ref, down_ref, ra_ref, up_ref,
    band_ref, col_ref, pa_ref, pb_ref,
    north, south, tile, col, far,
):
    even_lat = lax.rem(lax.axis_index("lat"), 2) == 0
    even_lon = lax.rem(lax.axis_index("lon"), 2) == 0

    @pl.when(even_lat)
    def _():
        south[...] = ra_ref[...]
        north[...] = down_ref[...]

    @pl.when(jnp.logical_not(even_lat))
    def _():
        north[...] = ra_ref[...]
        south[...] = up_ref[...]

    base = EDGE * SLABS
    col[HALO : HALO + ROWS + 16] = edge_ref[...].astype(F32)
    n_edge = north[base + 16 : base + 32].astype(F32)
    s_edge = south[base : base + 16].astype(F32)
    col[0:HALO] = n_edge[0:HALO]
    col[HALO : HALO + 1] += n_edge[HALO : HALO + 1]
    col[HALO + ROWS : HALO + ROWS + 1] += s_edge[0:1]
    col[HALO + ROWS + 1 : EXT_R] = s_edge[1:HALO]
    col_ref[...] = col[...].astype(BF16)

    above = north[base : base + 16].astype(F32)
    below = below_ref[...].astype(F32)
    for q in range(SLABS):
        cells = slice(GROUP * q, GROUP * (q + 1))
        tile[0, q] = own_ref[q, 0:16].astype(F32)
        tile[1, q] = south[EDGE * q : EDGE * q + 16].astype(F32)
        tile[0, q, 0:GROUP] += above[cells]
        tile[1, q, 0:GROUP] += below[cells]
        top, bottom = tile[0, q], tile[1, q]
        if q > 0:
            top, bottom = resolved(top), resolved(bottom)
        band_ref[q, 0:EDGE] = north[EDGE * q : EDGE * (q + 1)]
        band_ref[q, EDGE : EDGE + 16] = top.astype(BF16)
        band_ref[q, EDGE + 16 : EDGE + OWN] = own_ref[q, 16:OWN]
        band_ref[q, EDGE + OWN : EDGE + OWN + 16] = bottom.astype(BF16)
        band_ref[q, EDGE + OWN + 16 : EXT] = south[EDGE * q + 16 : EDGE * (q + 1)]

    def write(east_ref, west_ref):
        for k in range(HALO_SLABS):
            east_ref[EXT * k : EXT * (k + 1)] = band_ref[SLABS - HALO_SLABS + k]
            west_ref[EXT * k : EXT * (k + 1)] = band_ref[k]
        east_ref[EXT * HALO_SLABS :] = col_ref[...]
        west_ref[EXT * HALO_SLABS :] = jnp.zeros_like(col_ref)

    @pl.when(even_lon)
    def _():
        write(pa_ref, far)

    @pl.when(jnp.logical_not(even_lon))
    def _():
        write(far, pa_ref)

    pb_ref[...] = far[...]


def gelu(x):
    return 0.5 * x * (1.0 + lax.erf(x * (0.5**0.5)))


def half_sums(
    side_west, band_ref, col_ref, from_west, from_east, w1_ref, b1_ref, w2_ref, load, sums, emit,
    west_col, joined, ext, hidden, hidden_rest, w1_rest, w2_rest,
):
    lat = lax.axis_index("lat")
    last = lax.axis_size("lat") - 1
    out_ch = b1_ref.shape[1]
    side_east = jnp.logical_not(side_west)
    halves = [slice(h * LANES, (h + 1) * LANES) for h in range(2)]
    firsts = pl.ds(0, EXT_R, stride=GROUP)

    @pl.when(side_west)
    def _():
        west_col[...] = from_west[EXT * HALO_SLABS :].astype(F32)
        for k in range(HALO_SLABS):
            ext[k] = from_west[EXT * k : EXT * (k + 1)]
        for k in range(1, HALO_SLABS):
            ext[HALO_SLABS + k] = band_ref[k]
        for h, at in enumerate(halves):
            joined[h] = band_ref[0, :, at].astype(F32)

    @pl.when(side_east)
    def _():
        west_col[...] = col_ref[...].astype(F32)
        for k in range(1, HALO_SLABS):
            ext[HALO_SLABS + k] = from_east[EXT * k : EXT * (k + 1)]
        for k in range(HALO_SLABS):
            ext[k] = band_ref[k + 1]
        for h, at in enumerate(halves):
            joined[h] = from_east[0:EXT, at].astype(F32)

    for h, at in enumerate(halves):
        joined[h, firsts, :] += west_col[0:EXT_R, at]
        ext[HALO_SLABS, :, at] = resolved(joined[h]).astype(BF16)

    place = lax.broadcasted_iota(jnp.int32, (HID, 1), 0)
    inside = jnp.logical_and(
        jnp.logical_or(place >= 8 * GROUP, lat > 0),
        jnp.logical_or(place < HID - 8 * GROUP, lat < last),
    )
    rest = out_ch - MAIN
    w1_rest[...] = jnp.zeros_like(w1_rest)
    for a in range(3):
        for b in range(3):
            w1_rest[b, :, PAD * a : PAD * a + rest] = w1_ref[a, b, :, MAIN:]
    bias = b1_ref[:, :MAIN]
    bias_rest = jnp.concatenate([b1_ref[:, MAIN:], jnp.zeros((1, PAD - rest), F32)], axis=1)
    shift, reach = 4 * GROUP, 8 * GROUP
    for k in range(SIDE):
        total = jnp.zeros((HID, MAIN), F32) + bias
        tail = jnp.zeros((EXT, 3 * PAD), F32)
        for b in range(3):
            for a in range(3):
                piece = ext[k + b, shift * a : shift * a + HID]
                total = total + jnp.dot(
                    piece, w1_ref[a, b, :, :MAIN], preferred_element_type=F32
                )
            tail = tail + jnp.dot(ext[k + b], w1_rest[b], preferred_element_type=F32)
        total_rest = bias_rest
        for a in range(3):
            total_rest = total_rest + tail[shift * a : shift * a + HID, PAD * a : PAD * (a + 1)]
        hidden[k] = jnp.where(inside, gelu(total), 0.0).astype(BF16)
        value = jnp.where(inside, gelu(total_rest), 0.0)
        for a in range(3):
            hidden_rest[k, :, PAD * a : PAD * (a + 1)] = value[
                reach * a : reach * a + OWN
            ].astype(BF16)

    load.wait()
    w2_rest[...] = jnp.zeros_like(w2_rest)
    for a in range(3):
        for b in range(3):
            w2_rest[b, PAD * a : PAD * a + rest] = w2_ref[a, b, MAIN:]

    def second(first_slab):
        for k in range(SLABS):
            total = sums[k]
            for b in range(3):
                slab = k + 2 * b - first_slab
                if slab < 0 or slab >= SIDE:
                    continue
                for a in range(3):
                    piece = hidden[slab, reach * a : reach * a + OWN]
                    total = total + jnp.dot(
                        piece, w2_ref[a, b, :MAIN], preferred_element_type=F32
                    )
                total = total + jnp.dot(
                    hidden_rest[slab], w2_rest[b], preferred_element_type=F32
                )
            emit(k, total)

    @pl.when(side_west)
    def _():
        second(0)

    @pl.when(side_east)
    def _():
        second(SIDE)


def near_kernel(
    band_ref, col_ref, both_ref, w1_ref, b1_ref, w2_hbm, b2_ref,
    sums_ref,
    w2_ref, w2_sem, west_col, joined, ext, hidden, hidden_rest, w1_rest, w2_rest,
):
    load = pltpu.make_async_copy(w2_hbm, w2_ref, w2_sem)
    load.start()
    start = jnp.broadcast_to(b2_ref[...], sums_ref.shape[1:])

    def emit(k, total):
        sums_ref[k] = total

    odd = lax.rem(lax.axis_index("lon"), 2) == 1
    half_sums(
        odd, band_ref, col_ref, both_ref.at[0], both_ref.at[1], w1_ref, b1_ref, w2_ref, load, [start] * SLABS, emit,
        west_col, joined, ext, hidden, hidden_rest, w1_rest, w2_rest,
    )


def far_kernel(
    band_ref, col_ref, far_ref, w1_ref, b1_ref, w2_hbm, near_ref, keep_ref,
    out_ref,
    w2_ref, w2_sem, west_col, joined, ext, hidden, hidden_rest, w1_rest, w2_rest,
):
    load = pltpu.make_async_copy(w2_hbm, w2_ref, w2_sem)
    load.start()
    out_ch = b1_ref.shape[1]

    def emit(k, total):
        kept = keep_ref[k]
        kept = jnp.concatenate([kept] * pl.cdiv(out_ch, LANES), axis=1)[:, :out_ch]
        value = (gelu(total) * kept).reshape(ROWS, GROUP, out_ch)
        out_ref[:, GROUP * k : GROUP * (k + 1), :] = value

    even = lax.rem(lax.axis_index("lon"), 2) == 0
    half_sums(
        even, band_ref, col_ref, far_ref, far_ref, w1_ref, b1_ref, w2_ref, load, near_ref, emit,
        west_col, joined, ext, hidden, hidden_rest, w1_rest, w2_rest,
    )


def partners(axis, start, periodic):
    count = lax.axis_size(axis)
    route = []
    for i in range(start, count, 2):
        j = i + 1
        if j == count and not periodic:
            continue
        route += [(i, j % count), (j % count, i)]
    return route


def in_hbm(array):
    return pltpu.with_memory_space_constraint(array, pltpu.HBM)


def on_device(fields, land_sea, w_depth, b_depth, w_one, b_one, w_two, b_two):
    chans = fields.shape[2]
    out_ch = w_one.shape[3]
    vmem = pl.BlockSpec(memory_space=pltpu.VMEM)
    hbm = pl.BlockSpec(memory_space=pltpu.HBM)

    def shape(*dims, dtype=BF16):
        return jax.ShapeDtypeStruct(dims, dtype)

    lat_rows = SLABS * EDGE + 32
    lon_rows = HALO_SLABS * EXT + 64
    own, below, edge, keep, to_south, to_partner, to_north = pl.pallas_call(
        down_kernel,
        out_shape=(
            shape(SLABS, OWN, chans),
            shape(COLS, chans),
            shape(ROWS + 16, chans),
            shape(SLABS, OWN, LANES, dtype=F32),
            shape(lat_rows, chans),
            shape(lat_rows, chans),
            shape(lat_rows, chans),
        ),
        in_specs=[hbm] * 4,
        out_specs=[vmem] * 7,
        scratch_shapes=[
            pltpu.VMEM((2, 2 * ROWS, 2 * COLS, LANES), F32),
            pltpu.VMEM((COLS, ROWS), jnp.int32),
            pltpu.VMEM(w_depth.shape, F32),
            pltpu.VMEM((1, chans), F32),
            pltpu.SemaphoreType.DMA((2, CHUNKS)),
            pltpu.SemaphoreType.DMA((3,)),
            pltpu.VMEM((ROWS * COLS, LANES), F32),
            pltpu.VMEM((SLABS, OWN, chans), F32),
            pltpu.VMEM((ROWS + 16, chans), F32),
        ],
        compiler_params=pltpu.CompilerParams(vmem_limit_bytes=10 << 20),
        name="down",
    )(in_hbm(fields), in_hbm(land_sea.T), in_hbm(w_depth), in_hbm(b_depth[None]))

    swaps = partners("lat", 1, False)
    got_down = lax.ppermute(to_south, "lat", [(i, j) for i, j in swaps if i < j])
    got_a = lax.ppermute(to_partner, "lat", partners("lat", 0, False))
    got_up = lax.ppermute(to_north, "lat", [(i, j) for i, j in swaps if i > j])

    w_one = with_layout_constraint(w_one, Layout((0, 1, 2, 3)))
    got_down, w_one = lax.optimization_barrier((got_down, w_one))

    band, col, lon_a, lon_b = pl.pallas_call(
        band_kernel,
        out_shape=(
            shape(SLABS, EXT, chans),
            shape(64, chans),
            shape(lon_rows, chans),
            shape(lon_rows, chans),
        ),
        in_specs=[vmem] * 6,
        out_specs=[vmem] * 4,
        scratch_shapes=[
            pltpu.VMEM((lat_rows, chans), BF16),
            pltpu.VMEM((lat_rows, chans), BF16),
            pltpu.VMEM((2, SLABS, 16, chans), F32),
            pltpu.VMEM((64, chans), F32),
            pltpu.VMEM((lon_rows, chans), BF16),
        ],
        compiler_params=pltpu.CompilerParams(vmem_limit_bytes=10 << 20),
        name="band",
    )(own, below, edge, got_down, got_a, got_up)

    got_b = lax.ppermute(lon_b, "lon", partners("lon", 1, True))
    count = lax.axis_size("lon")
    chips = [[i, i + 1] for i in range(0, count, 2)]
    both = lax.all_gather(lon_a, "lon", axis_index_groups=chips)

    scratch = [
        pltpu.VMEM(w_two.shape, BF16),
        pltpu.SemaphoreType.DMA,
        pltpu.VMEM((64, chans), F32),
        pltpu.VMEM((2, EXT, LANES), F32),
        pltpu.VMEM((2 * HALO_SLABS, EXT, chans), BF16),
        pltpu.VMEM((SIDE, HID, MAIN), BF16),
        pltpu.VMEM((SIDE, OWN, 3 * PAD), BF16),
        pltpu.VMEM((3, chans, 3 * PAD), BF16),
        pltpu.VMEM((3, 3 * PAD, out_ch), BF16),
    ]
    w_two, b_one = in_hbm(w_two), b_one[None]
    flops = 2 * SIDE * HID * 9 * chans * out_ch + 2 * 6 * OWN * 3 * out_ch * out_ch
    cost = pl.CostEstimate(flops=flops, bytes_accessed=4 << 20, transcendentals=SIDE * HID * out_ch)
    near = pl.pallas_call(
        near_kernel,
        out_shape=shape(SLABS, OWN, out_ch, dtype=F32),
        in_specs=[vmem] * 5 + [hbm, vmem],
        out_specs=vmem,
        scratch_shapes=scratch,
        compiler_params=pltpu.CompilerParams(vmem_limit_bytes=14 << 20),
        cost_estimate=cost,
        name="near_half",
    )(band, col, both, w_one, b_one, w_two, b_two[None])

    return pl.pallas_call(
        far_kernel,
        out_shape=shape(ROWS, COLS, out_ch, dtype=F32),
        in_specs=[vmem] * 5 + [hbm, vmem, vmem],
        out_specs=vmem,
        scratch_shapes=scratch,
        compiler_params=pltpu.CompilerParams(vmem_limit_bytes=14 << 20),
        cost_estimate=cost,
        name="far_half",
    )(band, col, got_b, w_one, b_one, w_two, near, keep)


def solution(mesh):
    return jax.shard_map(
        on_device,
        mesh=mesh,
        in_specs=(P("lat", "lon", None), P("lat", "lon"), P(), P(), P(), P(), P(), P()),
        out_specs=P("lat", "lon", None),
        check_vma=False,
    )
```

```python
import jax
import jax.numpy as jnp
from jax import lax
from jax.experimental import pallas as pl
from jax.experimental.pallas import tpu as pltpu
from jax.sharding import PartitionSpec as P

ROWS = 32
COLS = 16
HALO = 12
GROUP = 4
SLABS = COLS // GROUP
HALO_SLABS = HALO // GROUP
OWN = ROWS * GROUP
EXT_R = ROWS + 2 * HALO
EXT = EXT_R * GROUP
HID = (ROWS + 16) * GROUP
SIDE = (COLS + 16) // GROUP // 2
EDGE = HALO * GROUP
EARLY = OWN - 16
LATE = EXT - EARLY
LANES = 128
MAIN = 256
PAD = 64
CHUNKS = 4
MASKED = 2.0**100
LIMIT = 2.0**90
F32 = jnp.float32
BF16 = jnp.bfloat16


def resolved(x):
    return jnp.where(x > LIMIT, 0.0, x)


def down_kernel(
    f_hbm, ls_hbm, wd_hbm, bd_hbm,
    own_ref, below_ref, edge_ref, keep_ref, south_ref, pa_ref, north_ref,
    f_ref, ls_ref, wd_ref, bd_ref, f_sem, sems, mask, patch, edge,
):
    lat = lax.axis_index("lat")
    last = lat == lax.axis_size("lat") - 1
    small = [
        pltpu.make_async_copy(src, dst, sems.at[k])
        for k, (src, dst) in enumerate(((ls_hbm, ls_ref), (wd_hbm, wd_ref), (bd_hbm, bd_ref)))
    ]
    for copy in small:
        copy.start()
    tall = 2 * ROWS // CHUNKS
    copies = {}
    for h in range(2):
        for k in range(CHUNKS):
            copies[h, k] = pltpu.make_async_copy(
                f_hbm.at[pl.ds(k * tall, tall), :, pl.ds(h * LANES, LANES)],
                f_ref.at[h, pl.ds(k * tall, tall)],
                f_sem.at[h, k],
            )
            copies[h, k].start()
    for copy in small:
        copy.wait()

    sea = ls_ref[...].astype(F32)
    for i in range(ROWS):
        mask[COLS * i : COLS * (i + 1)] = jnp.broadcast_to(sea[:, i : i + 1], (COLS, LANES))
    edge[...] = jnp.zeros_like(edge)

    first = lax.broadcasted_iota(jnp.int32, (COLS, LANES), 0) == 0
    holed = jnp.where(first, MASKED, 0.0)
    scale = jnp.where(last, 0.0, 1.0)
    for h in range(2):
        at = slice(h * LANES, (h + 1) * LANES)
        weight = [
            [jnp.broadcast_to(wd_ref[a, b : b + 1, at], (COLS, LANES)) for b in range(3)]
            for a in range(3)
        ]
        bias = jnp.broadcast_to(bd_ref[:, at], (COLS, LANES))
        for i in range(ROWS + 1):
            if i < ROWS and (2 * i) % tall == 0:
                copies[h, 2 * i // tall].wait()
            here, after = None, None
            for a in range(3):
                r = 2 * i - 1 + a
                if r < 0 or r >= 2 * ROWS:
                    continue
                even = f_ref[h, r, pl.ds(0, COLS, stride=2), :]
                odd = f_ref[h, r, pl.ds(1, COLS, stride=2), :]
                p = even * weight[a][1] + odd * weight[a][2]
                q = odd * weight[a][0]
                here = p if here is None else here + p
                after = q if after is None else after + q
            if i == ROWS:
                here, after = here * scale, after * scale
            else:
                here = here + bias
            moved = pltpu.roll(after, 1, 0)
            edge[i : i + 1, at] = moved[0:1]
            value = here + jnp.where(first, 0.0, moved)
            if i == ROWS:
                below_ref[:, at] = value.astype(BF16)
                continue
            kept = mask[COLS * i : COLS * (i + 1)]
            value = jnp.where(kept > 0.5, value, MASKED if i == 0 else holed)
            for q in range(SLABS):
                cells = slice(GROUP * i, GROUP * (i + 1))
                patch[q, cells, at] = value[GROUP * q : GROUP * (q + 1)]
                if h == 0:
                    keep_ref[q, cells] = kept[GROUP * q : GROUP * (q + 1)]

    own_ref[...] = patch[...].astype(BF16)
    edge_ref[...] = edge[...].astype(BF16)

    for q in range(SLABS):
        south_ref[EDGE * q : EDGE * (q + 1)] = own_ref[q, OWN - EDGE : OWN]
        north_ref[EDGE * q : EDGE * (q + 1)] = own_ref[q, 0:EDGE]
    base = EDGE * SLABS
    south_ref[base : base + 16] = below_ref[...]
    south_ref[base + 16 : base + 32] = edge[ROWS - HALO : ROWS - HALO + 16].astype(BF16)
    north_ref[base : base + 16] = edge[0:16].astype(BF16)
    north_ref[base + 16 : base + 32] = jnp.zeros((16, 2 * LANES), BF16)

    even = lax.rem(lat, 2) == 0

    @pl.when(even)
    def _():
        pa_ref[...] = south_ref[...]

    @pl.when(jnp.logical_not(even))
    def _():
        pa_ref[...] = north_ref[...]


def early_kernel(own_ref, edge_ref, early_ref, edge):
    even = lax.rem(lax.axis_index("lon"), 2) == 0
    edge[...] = edge_ref[...].astype(F32)
    base = EARLY * HALO_SLABS

    @pl.when(even)
    def _():
        for k in range(HALO_SLABS):
            early_ref[EARLY * k : EARLY * (k + 1)] = own_ref[k, 16:OWN]
        early_ref[base:] = jnp.zeros_like(early_ref[base:])

    @pl.when(jnp.logical_not(even))
    def _():
        for k in range(HALO_SLABS):
            early_ref[EARLY * k : EARLY * (k + 1)] = own_ref[SLABS - HALO_SLABS + k, 16:OWN]
        early_ref[base:] = edge[4:36].astype(BF16)


def band_kernel(
    own_ref, below_ref, edge_ref, down_ref, ra_ref, up_ref,
    band_ref, col_ref, pa_ref, pb_ref,
    north, south, tile, col,
):
    even_lat = lax.rem(lax.axis_index("lat"), 2) == 0
    even_lon = lax.rem(lax.axis_index("lon"), 2) == 0

    @pl.when(even_lat)
    def _():
        south[...] = ra_ref[...]
        north[...] = down_ref[...]

    @pl.when(jnp.logical_not(even_lat))
    def _():
        north[...] = ra_ref[...]
        south[...] = up_ref[...]

    base = EDGE * SLABS
    col[HALO : HALO + ROWS + 16] = edge_ref[...].astype(F32)
    n_edge = north[base + 16 : base + 32].astype(F32)
    s_edge = south[base : base + 16].astype(F32)
    col[0:HALO] = n_edge[0:HALO]
    col[HALO : HALO + 1] += n_edge[HALO : HALO + 1]
    col[HALO + ROWS : HALO + ROWS + 1] += s_edge[0:1]
    col[HALO + ROWS + 1 : EXT_R] = s_edge[1:HALO]
    col_ref[...] = col[...].astype(BF16)

    above = north[base : base + 16].astype(F32)
    below = below_ref[...].astype(F32)
    for q in range(SLABS):
        cells = slice(GROUP * q, GROUP * (q + 1))
        tile[0, q] = own_ref[q, 0:16].astype(F32)
        tile[1, q] = south[EDGE * q : EDGE * q + 16].astype(F32)
        tile[0, q, 0:GROUP] += above[cells]
        tile[1, q, 0:GROUP] += below[cells]
        top, bottom = tile[0, q], tile[1, q]
        if q > 0:
            top, bottom = resolved(top), resolved(bottom)
        band_ref[q, 0:EDGE] = north[EDGE * q : EDGE * (q + 1)]
        band_ref[q, EDGE : EDGE + 16] = top.astype(BF16)
        band_ref[q, EDGE + 16 : EDGE + OWN] = own_ref[q, 16:OWN]
        band_ref[q, EDGE + OWN : EDGE + OWN + 16] = bottom.astype(BF16)
        band_ref[q, EDGE + OWN + 16 : EXT] = south[EDGE * q + 16 : EDGE * (q + 1)]

    def write(east_ref, west_ref):
        top, late = 64, LATE - 64
        for k in range(HALO_SLABS):
            for ref, q, full in (
                (east_ref, SLABS - HALO_SLABS + k, east_ref is pa_ref),
                (west_ref, k, west_ref is pa_ref),
            ):
                if full:
                    ref[EXT * k : EXT * (k + 1)] = band_ref[q]
                else:
                    ref[LATE * k : LATE * k + top] = band_ref[q, 0:top]
                    ref[LATE * k + top : LATE * (k + 1)] = band_ref[q, EXT - late : EXT]
        if east_ref is pa_ref:
            east_ref[EXT * HALO_SLABS :] = col_ref[...]
            west_ref[LATE * HALO_SLABS :] = jnp.zeros_like(west_ref[LATE * HALO_SLABS :])
        else:
            base = LATE * HALO_SLABS
            east_ref[base : base + 16] = col[0:16].astype(BF16)
            east_ref[base + 16 : base + 32] = col[EXT_R - HALO : EXT_R + 4].astype(BF16)
            west_ref[EXT * HALO_SLABS :] = jnp.zeros_like(col_ref)

    @pl.when(even_lon)
    def _():
        write(pa_ref, pb_ref)

    @pl.when(jnp.logical_not(even_lon))
    def _():
        write(pb_ref, pa_ref)


def gelu(x):
    return 0.5 * x * (1.0 + lax.erf(x * (0.5**0.5)))


def half_sums(
    side_west, band_ref, col_ref, from_west, from_east, w1_ref, w1_rest, b1_ref, w2_ref, load, sums, emit,
    west_col, joined, ext, hidden, hidden_rest, w2_rest,
):
    lat = lax.axis_index("lat")
    last = lax.axis_size("lat") - 1
    out_ch = b1_ref.shape[1]
    side_east = jnp.logical_not(side_west)
    halves = [slice(h * LANES, (h + 1) * LANES) for h in range(2)]
    firsts = pl.ds(0, EXT_R, stride=GROUP)

    @pl.when(side_west)
    def _():
        west_col[...] = from_west[EXT * HALO_SLABS :].astype(F32)
        for k in range(HALO_SLABS):
            ext[k] = from_west[EXT * k : EXT * (k + 1)]
        for k in range(1, HALO_SLABS):
            ext[HALO_SLABS + k] = band_ref[k]
        for h, at in enumerate(halves):
            joined[h] = band_ref[0, :, at].astype(F32)

    @pl.when(side_east)
    def _():
        west_col[...] = col_ref[...].astype(F32)
        for k in range(1, HALO_SLABS):
            ext[HALO_SLABS + k] = from_east[EXT * k : EXT * (k + 1)]
        for k in range(HALO_SLABS):
            ext[k] = band_ref[k + 1]
        for h, at in enumerate(halves):
            joined[h] = from_east[0:EXT, at].astype(F32)

    for h, at in enumerate(halves):
        joined[h, firsts, :] += west_col[0:EXT_R, at]
        ext[HALO_SLABS, :, at] = resolved(joined[h]).astype(BF16)

    place = lax.broadcasted_iota(jnp.int32, (HID, 1), 0)
    inside = jnp.logical_and(
        jnp.logical_or(place >= 8 * GROUP, lat > 0),
        jnp.logical_or(place < HID - 8 * GROUP, lat < last),
    )
    rest = out_ch - MAIN
    bias = b1_ref[:, :MAIN]
    bias_rest = jnp.concatenate([b1_ref[:, MAIN:], jnp.zeros((1, PAD - rest), F32)], axis=1)
    shift, reach = 4 * GROUP, 8 * GROUP
    for k in range(SIDE):
        total = jnp.zeros((HID, MAIN), F32) + bias
        tail = jnp.zeros((EXT, MAIN), F32)
        for b in range(3):
            for a in range(3):
                piece = ext[k + b, shift * a : shift * a + HID]
                total = total + jnp.dot(
                    piece, w1_ref[a, b], preferred_element_type=F32
                )
            tail = tail + jnp.dot(ext[k + b], w1_rest[b], preferred_element_type=F32)
        total_rest = bias_rest
        for a in range(3):
            total_rest = total_rest + tail[shift * a : shift * a + HID, PAD * a : PAD * (a + 1)]
        hidden[k] = jnp.where(inside, gelu(total), 0.0).astype(BF16)
        value = jnp.where(inside, gelu(total_rest), 0.0)
        for a in range(3):
            hidden_rest[k, :, PAD * a : PAD * (a + 1)] = value[
                reach * a : reach * a + OWN
            ].astype(BF16)

    load.wait()
    w2_rest[...] = jnp.zeros_like(w2_rest)
    for a in range(3):
        for b in range(3):
            w2_rest[b, PAD * a : PAD * a + rest] = w2_ref[a, b, MAIN:]

    def second(first_slab):
        for k in range(SLABS):
            total = sums[k]
            for b in range(3):
                slab = k + 2 * b - first_slab
                if slab < 0 or slab >= SIDE:
                    continue
                for a in range(3):
                    piece = hidden[slab, reach * a : reach * a + OWN]
                    total = total + jnp.dot(
                        piece, w2_ref[a, b, :MAIN], preferred_element_type=F32
                    )
                total = total + jnp.dot(
                    hidden_rest[slab], w2_rest[b], preferred_element_type=F32
                )
            emit(k, total)

    @pl.when(side_west)
    def _():
        second(0)

    @pl.when(side_east)
    def _():
        second(SIDE)


def near_kernel(
    band_ref, col_ref, both_ref, stored_ref, b1_ref, w2_hbm, b2_ref,
    sums_ref, w1_ref, w1_rest,
    w2_ref, w2_sem, west_col, joined, ext, hidden, hidden_rest, w2_rest, stack,
):
    load = pltpu.make_async_copy(w2_hbm, w2_ref, w2_sem)
    load.start()
    rest = stored_ref.shape[2] - MAIN
    stack[...] = jnp.zeros_like(stack)
    for b in range(3):
        for a in range(3):
            w1_ref[a, b] = stored_ref[a, b, :MAIN].T
            stack[b, PAD * a : PAD * a + rest] = stored_ref[a, b, MAIN:]
        w1_rest[b] = stack[b].T
    start = jnp.broadcast_to(b2_ref[...], sums_ref.shape[1:])

    def emit(k, total):
        sums_ref[k] = total

    odd = lax.rem(lax.axis_index("lon"), 2) == 1
    half_sums(
        odd, band_ref, col_ref, both_ref.at[0], both_ref.at[1], w1_ref, w1_rest, b1_ref, w2_ref, load, [start] * SLABS, emit,
        west_col, joined, ext, hidden, hidden_rest, w2_rest,
    )


def far_kernel(
    band_ref, col_ref, early_ref, late_ref, w1_ref, w1_rest, b1_ref, w2_hbm, near_ref, keep_ref,
    out_ref,
    w2_ref, w2_sem, west_col, joined, ext, hidden, hidden_rest, w2_rest, far_ref, far_col,
):
    load = pltpu.make_async_copy(w2_hbm, w2_ref, w2_sem)
    load.start()
    out_ch = b1_ref.shape[1]
    for k in range(HALO_SLABS):
        at = EXT * k
        far_ref[at : at + 64] = late_ref[LATE * k : LATE * k + 64]
        far_ref[at + 64 : at + 64 + EARLY] = early_ref[EARLY * k : EARLY * (k + 1)]
        far_ref[at + 64 + EARLY : at + EXT] = late_ref[LATE * k + 64 : LATE * (k + 1)]
    base = LATE * HALO_SLABS
    far_col[0:16] = late_ref[base : base + 16].astype(F32)
    far_col[16:48] = early_ref[EARLY * HALO_SLABS :].astype(F32)
    far_col[EXT_R - HALO : EXT_R + 4] = late_ref[base + 16 : base + 32].astype(F32)
    far_col[EXT_R + 4 :] = jnp.zeros_like(far_col[EXT_R + 4 :])
    far_ref[EXT * HALO_SLABS :] = far_col[...].astype(BF16)

    def emit(k, total):
        kept = keep_ref[k]
        kept = jnp.concatenate([kept] * pl.cdiv(out_ch, LANES), axis=1)[:, :out_ch]
        value = (gelu(total) * kept).reshape(ROWS, GROUP, out_ch)
        out_ref[:, GROUP * k : GROUP * (k + 1), :] = value

    even = lax.rem(lax.axis_index("lon"), 2) == 0
    half_sums(
        even, band_ref, col_ref, far_ref, far_ref, w1_ref, w1_rest, b1_ref, w2_ref, load, near_ref, emit,
        west_col, joined, ext, hidden, hidden_rest, w2_rest,
    )


def partners(axis, start, periodic):
    count = lax.axis_size(axis)
    route = []
    for i in range(start, count, 2):
        j = i + 1
        if j == count and not periodic:
            continue
        route += [(i, j % count), (j % count, i)]
    return route


def in_hbm(array):
    return pltpu.with_memory_space_constraint(array, pltpu.HBM)


def on_device(fields, land_sea, w_depth, b_depth, w_one, b_one, w_two, b_two):
    chans = fields.shape[2]
    out_ch = w_one.shape[3]
    vmem = pl.BlockSpec(memory_space=pltpu.VMEM)
    hbm = pl.BlockSpec(memory_space=pltpu.HBM)

    def shape(*dims, dtype=BF16):
        return jax.ShapeDtypeStruct(dims, dtype)

    lat_rows = SLABS * EDGE + 32
    lon_rows = HALO_SLABS * EXT + 64
    own, below, edge, keep, to_south, to_partner, to_north = pl.pallas_call(
        down_kernel,
        out_shape=(
            shape(SLABS, OWN, chans),
            shape(COLS, chans),
            shape(ROWS + 16, chans),
            shape(SLABS, OWN, LANES, dtype=F32),
            shape(lat_rows, chans),
            shape(lat_rows, chans),
            shape(lat_rows, chans),
        ),
        in_specs=[hbm] * 4,
        out_specs=[vmem] * 7,
        scratch_shapes=[
            pltpu.VMEM((2, 2 * ROWS, 2 * COLS, LANES), F32),
            pltpu.VMEM((COLS, ROWS), jnp.int32),
            pltpu.VMEM(w_depth.shape, F32),
            pltpu.VMEM((1, chans), F32),
            pltpu.SemaphoreType.DMA((2, CHUNKS)),
            pltpu.SemaphoreType.DMA((3,)),
            pltpu.VMEM((ROWS * COLS, LANES), F32),
            pltpu.VMEM((SLABS, OWN, chans), F32),
            pltpu.VMEM((ROWS + 16, chans), F32),
        ],
        compiler_params=pltpu.CompilerParams(vmem_limit_bytes=10 << 20),
        name="down",
    )(in_hbm(fields), in_hbm(land_sea.T), in_hbm(w_depth), in_hbm(b_depth[None]))

    swaps = partners("lat", 1, False)
    got_down = lax.ppermute(to_south, "lat", [(i, j) for i, j in swaps if i < j])
    got_a = lax.ppermute(to_partner, "lat", partners("lat", 0, False))
    got_up = lax.ppermute(to_north, "lat", [(i, j) for i, j in swaps if i > j])

    early_rows = EARLY * HALO_SLABS + 32
    early = pl.pallas_call(
        early_kernel,
        out_shape=shape(early_rows, chans),
        in_specs=[vmem] * 2,
        out_specs=vmem,
        scratch_shapes=[pltpu.VMEM((ROWS + 16, chans), F32)],
        compiler_params=pltpu.CompilerParams(vmem_limit_bytes=4 << 20),
        name="early",
    )(own, edge)
    got_early = lax.ppermute(early, "lon", partners("lon", 1, True))

    band, col, lon_a, lon_b = pl.pallas_call(
        band_kernel,
        out_shape=(
            shape(SLABS, EXT, chans),
            shape(64, chans),
            shape(lon_rows, chans),
            shape(LATE * HALO_SLABS + 32, chans),
        ),
        in_specs=[vmem] * 6,
        out_specs=[vmem] * 4,
        scratch_shapes=[
            pltpu.VMEM((lat_rows, chans), BF16),
            pltpu.VMEM((lat_rows, chans), BF16),
            pltpu.VMEM((2, SLABS, 16, chans), F32),
            pltpu.VMEM((64, chans), F32),
        ],
        compiler_params=pltpu.CompilerParams(vmem_limit_bytes=10 << 20),
        name="band",
    )(own, below, edge, got_down, got_a, got_up)

    got_b = lax.ppermute(lon_b, "lon", partners("lon", 1, True))
    count = lax.axis_size("lon")
    chips = [[i, i + 1] for i in range(0, count, 2)]
    both = lax.all_gather(lon_a, "lon", axis_index_groups=chips)

    scratch = [
        pltpu.VMEM(w_two.shape, BF16),
        pltpu.SemaphoreType.DMA,
        pltpu.VMEM((64, chans), F32),
        pltpu.VMEM((2, EXT, LANES), F32),
        pltpu.VMEM((2 * HALO_SLABS, EXT, chans), BF16),
        pltpu.VMEM((SIDE, HID, MAIN), BF16),
        pltpu.VMEM((SIDE, OWN, 3 * PAD), BF16),
        pltpu.VMEM((3, 3 * PAD, out_ch), BF16),
    ]
    w_two, b_one = in_hbm(w_two), b_one[None]
    flops = 2 * SIDE * HID * 9 * chans * out_ch + 2 * 6 * OWN * 3 * out_ch * out_ch
    cost = pl.CostEstimate(flops=flops, bytes_accessed=4 << 20, transcendentals=SIDE * HID * out_ch)
    near, w1_main, w1_rest = pl.pallas_call(
        near_kernel,
        out_shape=(
            shape(SLABS, OWN, out_ch, dtype=F32),
            shape(3, 3, chans, MAIN),
            shape(3, chans, MAIN),
        ),
        in_specs=[vmem] * 5 + [hbm, vmem],
        out_specs=[vmem] * 3,
        scratch_shapes=scratch + [pltpu.VMEM((3, MAIN, chans), BF16)],
        compiler_params=pltpu.CompilerParams(vmem_limit_bytes=14 << 20),
        cost_estimate=cost,
        name="near_half",
    )(band, col, both, w_one.transpose(0, 1, 3, 2), b_one, w_two, b_two[None])

    return pl.pallas_call(
        far_kernel,
        out_shape=shape(ROWS, COLS, out_ch, dtype=F32),
        in_specs=[vmem] * 7 + [hbm, vmem, vmem],
        out_specs=vmem,
        scratch_shapes=scratch
        + [pltpu.VMEM((lon_rows, chans), BF16), pltpu.VMEM((64, chans), F32)],
        compiler_params=pltpu.CompilerParams(vmem_limit_bytes=14 << 20),
        cost_estimate=cost,
        name="far_half",
    )(band, col, got_early, got_b, w1_main, w1_rest, b_one, w_two, near, keep)


def solution(mesh):
    return jax.shard_map(
        on_device,
        mesh=mesh,
        in_specs=(P("lat", "lon", None), P("lat", "lon"), P(), P(), P(), P(), P(), P()),
        out_specs=P("lat", "lon", None),
        check_vma=False,
    )
```

```python
import jax
import jax.numpy as jnp
from jax import lax
from jax.experimental import pallas as pl
from jax.experimental.pallas import tpu as pltpu
from jax.sharding import PartitionSpec as P

ROWS = 32
COLS = 16
HALO = 12
GROUP = 4
SLABS = COLS // GROUP
HALO_SLABS = HALO // GROUP
OWN = ROWS * GROUP
EXT_R = ROWS + 2 * HALO
EXT = EXT_R * GROUP
HID = (ROWS + 16) * GROUP
SIDE = (COLS + 16) // GROUP // 2
EDGE = HALO * GROUP
EARLY = OWN - 16
LATE = EXT - EARLY
LANES = 128
MAIN = 256
PAD = 64
CHUNKS = 2
MASKED = 2.0**100
LIMIT = 2.0**90
F32 = jnp.float32
BF16 = jnp.bfloat16


def resolved(x):
    return jnp.where(x > LIMIT, 0.0, x)


def down_kernel(
    f_hbm, ls_hbm, wd_hbm, bd_hbm,
    own_ref, below_ref, edge_ref, keep_ref, south_ref, pa_ref, north_ref,
    f_ref, ls_ref, wd_ref, bd_ref, f_sem, sems, mask, patch, edge,
):
    lat = lax.axis_index("lat")
    last = lat == lax.axis_size("lat") - 1
    small = [
        pltpu.make_async_copy(src, dst, sems.at[k])
        for k, (src, dst) in enumerate(((ls_hbm, ls_ref), (wd_hbm, wd_ref), (bd_hbm, bd_ref)))
    ]
    for copy in small:
        copy.start()
    tall = 2 * ROWS // CHUNKS
    copies = {}
    for h in range(2):
        for k in range(CHUNKS):
            copies[h, k] = pltpu.make_async_copy(
                f_hbm.at[pl.ds(k * tall, tall), :, pl.ds(h * LANES, LANES)],
                f_ref.at[h, pl.ds(k * tall, tall)],
                f_sem.at[h, k],
            )
            copies[h, k].start()
    for copy in small:
        copy.wait()

    sea = ls_ref[...].astype(F32)
    for i in range(ROWS):
        mask[COLS * i : COLS * (i + 1)] = jnp.broadcast_to(sea[:, i : i + 1], (COLS, LANES))
    edge[...] = jnp.zeros_like(edge)

    first = lax.broadcasted_iota(jnp.int32, (COLS, LANES), 0) == 0
    holed = jnp.where(first, MASKED, 0.0)
    scale = jnp.where(last, 0.0, 1.0)
    for h in range(2):
        at = slice(h * LANES, (h + 1) * LANES)
        weight = [
            [jnp.broadcast_to(wd_ref[a, b : b + 1, at], (COLS, LANES)) for b in range(3)]
            for a in range(3)
        ]
        bias = jnp.broadcast_to(bd_ref[:, at], (COLS, LANES))
        for i in range(ROWS + 1):
            if i < ROWS and (2 * i) % tall == 0:
                copies[h, 2 * i // tall].wait()
            here, after = None, None
            for a in range(3):
                r = 2 * i - 1 + a
                if r < 0 or r >= 2 * ROWS:
                    continue
                even = f_ref[h, r, pl.ds(0, COLS, stride=2), :]
                odd = f_ref[h, r, pl.ds(1, COLS, stride=2), :]
                p = even * weight[a][1] + odd * weight[a][2]
                q = odd * weight[a][0]
                here = p if here is None else here + p
                after = q if after is None else after + q
            if i == ROWS:
                here, after = here * scale, after * scale
            else:
                here = here + bias
            moved = pltpu.roll(after, 1, 0)
            edge[i : i + 1, at] = moved[0:1]
            value = here + jnp.where(first, 0.0, moved)
            if i == ROWS:
                below_ref[:, at] = value.astype(BF16)
                continue
            kept = mask[COLS * i : COLS * (i + 1)]
            value = jnp.where(kept > 0.5, value, MASKED if i == 0 else holed)
            for q in range(SLABS):
                cells = slice(GROUP * i, GROUP * (i + 1))
                patch[q, cells, at] = value[GROUP * q : GROUP * (q + 1)]
                if h == 0:
                    keep_ref[q, cells] = kept[GROUP * q : GROUP * (q + 1)]

    own_ref[...] = patch[...].astype(BF16)
    edge_ref[...] = edge[...].astype(BF16)

    for q in range(SLABS):
        south_ref[EDGE * q : EDGE * (q + 1)] = own_ref[q, OWN - EDGE : OWN]
        north_ref[EDGE * q : EDGE * (q + 1)] = own_ref[q, 0:EDGE]
    base = EDGE * SLABS
    south_ref[base : base + 16] = below_ref[...]
    south_ref[base + 16 : base + 32] = edge[ROWS - HALO : ROWS - HALO + 16].astype(BF16)
    north_ref[base : base + 16] = edge[0:16].astype(BF16)
    north_ref[base + 16 : base + 32] = jnp.zeros((16, 2 * LANES), BF16)

    even = lax.rem(lat, 2) == 0

    @pl.when(even)
    def _():
        pa_ref[...] = south_ref[...]

    @pl.when(jnp.logical_not(even))
    def _():
        pa_ref[...] = north_ref[...]


def early_kernel(own_ref, edge_ref, early_ref, edge):
    even = lax.rem(lax.axis_index("lon"), 2) == 0
    edge[...] = edge_ref[...].astype(F32)
    base = EARLY * HALO_SLABS

    @pl.when(even)
    def _():
        for k in range(HALO_SLABS):
            early_ref[EARLY * k : EARLY * (k + 1)] = own_ref[k, 16:OWN]
        early_ref[base:] = jnp.zeros_like(early_ref[base:])

    @pl.when(jnp.logical_not(even))
    def _():
        for k in range(HALO_SLABS):
            early_ref[EARLY * k : EARLY * (k + 1)] = own_ref[SLABS - HALO_SLABS + k, 16:OWN]
        early_ref[base:] = edge[4:36].astype(BF16)


def band_kernel(
    own_ref, below_ref, edge_ref, down_ref, ra_ref, up_ref,
    band_ref, col_ref, pa_ref, pb_ref,
    north, south, tile, col,
):
    even_lat = lax.rem(lax.axis_index("lat"), 2) == 0
    even_lon = lax.rem(lax.axis_index("lon"), 2) == 0

    @pl.when(even_lat)
    def _():
        south[...] = ra_ref[...]
        north[...] = down_ref[...]

    @pl.when(jnp.logical_not(even_lat))
    def _():
        north[...] = ra_ref[...]
        south[...] = up_ref[...]

    base = EDGE * SLABS
    col[HALO : HALO + ROWS + 16] = edge_ref[...].astype(F32)
    n_edge = north[base + 16 : base + 32].astype(F32)
    s_edge = south[base : base + 16].astype(F32)
    col[0:HALO] = n_edge[0:HALO]
    col[HALO : HALO + 1] += n_edge[HALO : HALO + 1]
    col[HALO + ROWS : HALO + ROWS + 1] += s_edge[0:1]
    col[HALO + ROWS + 1 : EXT_R] = s_edge[1:HALO]
    col_ref[...] = col[...].astype(BF16)

    above = north[base : base + 16].astype(F32)
    below = below_ref[...].astype(F32)
    for q in range(SLABS):
        cells = slice(GROUP * q, GROUP * (q + 1))
        tile[0, q] = own_ref[q, 0:16].astype(F32)
        tile[1, q] = south[EDGE * q : EDGE * q + 16].astype(F32)
        tile[0, q, 0:GROUP] += above[cells]
        tile[1, q, 0:GROUP] += below[cells]
        top, bottom = tile[0, q], tile[1, q]
        if q > 0:
            top, bottom = resolved(top), resolved(bottom)
        band_ref[q, 0:EDGE] = north[EDGE * q : EDGE * (q + 1)]
        band_ref[q, EDGE : EDGE + 16] = top.astype(BF16)
        band_ref[q, EDGE + 16 : EDGE + OWN] = own_ref[q, 16:OWN]
        band_ref[q, EDGE + OWN : EDGE + OWN + 16] = bottom.astype(BF16)
        band_ref[q, EDGE + OWN + 16 : EXT] = south[EDGE * q + 16 : EDGE * (q + 1)]

    def write(east_ref, west_ref):
        top, late = 64, LATE - 64
        for k in range(HALO_SLABS):
            for ref, q, full in (
                (east_ref, SLABS - HALO_SLABS + k, east_ref is pa_ref),
                (west_ref, k, west_ref is pa_ref),
            ):
                if full:
                    ref[EXT * k : EXT * (k + 1)] = band_ref[q]
                else:
                    ref[LATE * k : LATE * k + top] = band_ref[q, 0:top]
                    ref[LATE * k + top : LATE * (k + 1)] = band_ref[q, EXT - late : EXT]
        if east_ref is pa_ref:
            east_ref[EXT * HALO_SLABS :] = col_ref[...]
            west_ref[LATE * HALO_SLABS :] = jnp.zeros_like(west_ref[LATE * HALO_SLABS :])
        else:
            base = LATE * HALO_SLABS
            east_ref[base : base + 16] = col[0:16].astype(BF16)
            east_ref[base + 16 : base + 32] = col[EXT_R - HALO : EXT_R + 4].astype(BF16)
            west_ref[EXT * HALO_SLABS :] = jnp.zeros_like(col_ref)

    @pl.when(even_lon)
    def _():
        write(pa_ref, pb_ref)

    @pl.when(jnp.logical_not(even_lon))
    def _():
        write(pb_ref, pa_ref)


def gelu(x):
    return 0.5 * x * (1.0 + lax.erf(x * (0.5**0.5)))


def half_sums(
    side_west, band_ref, col_ref, from_west, from_east, w1_ref, w1_rest, b1_ref, w2_ref, load, sums, emit,
    west_col, joined, ext, hidden, hidden_rest, w2_rest, gather,
):
    lat = lax.axis_index("lat")
    last = lax.axis_size("lat") - 1
    out_ch = b1_ref.shape[1]
    side_east = jnp.logical_not(side_west)
    halves = [slice(h * LANES, (h + 1) * LANES) for h in range(2)]
    firsts = pl.ds(0, EXT_R, stride=GROUP)

    @pl.when(side_west)
    def _():
        west_col[...] = from_west[EXT * HALO_SLABS :].astype(F32)
        for k in range(HALO_SLABS):
            ext[k] = from_west[EXT * k : EXT * (k + 1)]
        for k in range(1, HALO_SLABS):
            ext[HALO_SLABS + k] = band_ref[k]
        for h, at in enumerate(halves):
            joined[h] = band_ref[0, :, at].astype(F32)

    @pl.when(side_east)
    def _():
        west_col[...] = col_ref[...].astype(F32)
        for k in range(1, HALO_SLABS):
            ext[HALO_SLABS + k] = from_east[EXT * k : EXT * (k + 1)]
        for k in range(HALO_SLABS):
            ext[k] = band_ref[k + 1]
        for h, at in enumerate(halves):
            joined[h] = from_east[0:EXT, at].astype(F32)

    for h, at in enumerate(halves):
        joined[h, firsts, :] += west_col[0:EXT_R, at]
        ext[HALO_SLABS, :, at] = resolved(joined[h]).astype(BF16)

    place = lax.broadcasted_iota(jnp.int32, (HID, 1), 0)
    inside = jnp.logical_and(
        jnp.logical_or(place >= 8 * GROUP, lat > 0),
        jnp.logical_or(place < HID - 8 * GROUP, lat < last),
    )
    rest = out_ch - MAIN
    bias = b1_ref[:, :MAIN]
    bias_rest = jnp.concatenate([b1_ref[:, MAIN:], jnp.zeros((1, PAD - rest), F32)], axis=1)
    shift, reach = 4 * GROUP, 8 * GROUP
    for k in range(SIDE):
        total = jnp.zeros((HID, MAIN), F32) + bias
        tail = jnp.zeros((EXT, MAIN), F32)
        for b in range(3):
            for a in range(3):
                piece = ext[k + b, shift * a : shift * a + HID]
                total = total + jnp.dot(
                    piece, w1_ref[a, b], preferred_element_type=F32
                )
            tail = tail + jnp.dot(ext[k + b], w1_rest[b], preferred_element_type=F32)
        total_rest = bias_rest
        for a in range(3):
            total_rest = total_rest + tail[shift * a : shift * a + HID, PAD * a : PAD * (a + 1)]
        hidden[k] = jnp.where(inside, gelu(total), 0.0).astype(BF16)
        value = jnp.where(inside, gelu(total_rest), 0.0)
        for a in range(3):
            hidden_rest[k, :, PAD * a : PAD * (a + 1)] = value[
                reach * a : reach * a + OWN
            ].astype(BF16)

    load.wait()
    if gather:
        w2_rest[...] = jnp.zeros_like(w2_rest)
        for a in range(3):
            for b in range(3):
                w2_rest[b, PAD * a : PAD * a + rest] = w2_ref[a, b, MAIN:]

    def second(first_slab):
        for k in range(SLABS):
            total = sums[k]
            for b in range(3):
                slab = k + 2 * b - first_slab
                if slab < 0 or slab >= SIDE:
                    continue
                for a in range(3):
                    piece = hidden[slab, reach * a : reach * a + OWN]
                    total = total + jnp.dot(
                        piece, w2_ref[a, b, :MAIN], preferred_element_type=F32
                    )
                total = total + jnp.dot(
                    hidden_rest[slab], w2_rest[b], preferred_element_type=F32
                )
            emit(k, total)

    @pl.when(side_west)
    def _():
        second(0)

    @pl.when(side_east)
    def _():
        second(SIDE)


def near_kernel(
    band_ref, col_ref, both_ref, stored_ref, b1_ref, w2_hbm, b2_ref,
    sums_ref, w1_ref, w1_rest, w2_rest,
    w2_ref, w2_sem, west_col, joined, ext, hidden, hidden_rest, stack,
):
    load = pltpu.make_async_copy(w2_hbm, w2_ref, w2_sem)
    load.start()
    rest = stored_ref.shape[2] - MAIN
    stack[...] = jnp.zeros_like(stack)
    for b in range(3):
        for a in range(3):
            w1_ref[a, b] = stored_ref[a, b, :MAIN].T
            stack[b, PAD * a : PAD * a + rest] = stored_ref[a, b, MAIN:]
        w1_rest[b] = stack[b].T
    start = jnp.broadcast_to(b2_ref[...], sums_ref.shape[1:])

    def emit(k, total):
        sums_ref[k] = total

    odd = lax.rem(lax.axis_index("lon"), 2) == 1
    half_sums(
        odd, band_ref, col_ref, both_ref.at[0], both_ref.at[1], w1_ref, w1_rest, b1_ref, w2_ref, load, [start] * SLABS, emit,
        west_col, joined, ext, hidden, hidden_rest, w2_rest, True,
    )


def far_kernel(
    band_ref, col_ref, early_ref, late_ref, w1_ref, w1_rest, b1_ref, w2_hbm, near_ref, keep_ref, w2_rest,
    out_ref,
    w2_ref, w2_sem, west_col, joined, ext, hidden, hidden_rest, far_ref, far_col,
):
    load = pltpu.make_async_copy(w2_hbm, w2_ref, w2_sem)
    load.start()
    out_ch = b1_ref.shape[1]
    for k in range(HALO_SLABS):
        at = EXT * k
        far_ref[at : at + 64] = late_ref[LATE * k : LATE * k + 64]
        far_ref[at + 64 : at + 64 + EARLY] = early_ref[EARLY * k : EARLY * (k + 1)]
        far_ref[at + 64 + EARLY : at + EXT] = late_ref[LATE * k + 64 : LATE * (k + 1)]
    base = LATE * HALO_SLABS
    far_col[0:16] = late_ref[base : base + 16].astype(F32)
    far_col[16:48] = early_ref[EARLY * HALO_SLABS :].astype(F32)
    far_col[EXT_R - HALO : EXT_R + 4] = late_ref[base + 16 : base + 32].astype(F32)
    far_col[EXT_R + 4 :] = jnp.zeros_like(far_col[EXT_R + 4 :])
    far_ref[EXT * HALO_SLABS :] = far_col[...].astype(BF16)

    def emit(k, total):
        kept = keep_ref[k]
        kept = jnp.concatenate([kept] * pl.cdiv(out_ch, LANES), axis=1)[:, :out_ch]
        value = (gelu(total) * kept).reshape(ROWS, GROUP, out_ch)
        out_ref[:, GROUP * k : GROUP * (k + 1), :] = value

    even = lax.rem(lax.axis_index("lon"), 2) == 0
    half_sums(
        even, band_ref, col_ref, far_ref, far_ref, w1_ref, w1_rest, b1_ref, w2_ref, load, near_ref, emit,
        west_col, joined, ext, hidden, hidden_rest, w2_rest, False,
    )


def partners(axis, start, periodic):
    count = lax.axis_size(axis)
    route = []
    for i in range(start, count, 2):
        j = i + 1
        if j == count and not periodic:
            continue
        route += [(i, j % count), (j % count, i)]
    return route


def in_hbm(array):
    return pltpu.with_memory_space_constraint(array, pltpu.HBM)


def on_device(fields, land_sea, w_depth, b_depth, w_one, b_one, w_two, b_two):
    chans = fields.shape[2]
    out_ch = w_one.shape[3]
    vmem = pl.BlockSpec(memory_space=pltpu.VMEM)
    hbm = pl.BlockSpec(memory_space=pltpu.HBM)

    def shape(*dims, dtype=BF16):
        return jax.ShapeDtypeStruct(dims, dtype)

    lat_rows = SLABS * EDGE + 32
    lon_rows = HALO_SLABS * EXT + 64
    own, below, edge, keep, to_south, to_partner, to_north = pl.pallas_call(
        down_kernel,
        out_shape=(
            shape(SLABS, OWN, chans),
            shape(COLS, chans),
            shape(ROWS + 16, chans),
            shape(SLABS, OWN, LANES, dtype=F32),
            shape(lat_rows, chans),
            shape(lat_rows, chans),
            shape(lat_rows, chans),
        ),
        in_specs=[hbm] * 4,
        out_specs=[vmem] * 7,
        scratch_shapes=[
            pltpu.VMEM((2, 2 * ROWS, 2 * COLS, LANES), F32),
            pltpu.VMEM((COLS, ROWS), jnp.int32),
            pltpu.VMEM(w_depth.shape, F32),
            pltpu.VMEM((1, chans), F32),
            pltpu.SemaphoreType.DMA((2, CHUNKS)),
            pltpu.SemaphoreType.DMA((3,)),
            pltpu.VMEM((ROWS * COLS, LANES), F32),
            pltpu.VMEM((SLABS, OWN, chans), F32),
            pltpu.VMEM((ROWS + 16, chans), F32),
        ],
        compiler_params=pltpu.CompilerParams(vmem_limit_bytes=10 << 20),
        name="down",
    )(in_hbm(fields), in_hbm(land_sea.T), in_hbm(w_depth), in_hbm(b_depth[None]))

    swaps = partners("lat", 1, False)
    got_down = lax.ppermute(to_south, "lat", [(i, j) for i, j in swaps if i < j])
    got_a = lax.ppermute(to_partner, "lat", partners("lat", 0, False))
    got_up = lax.ppermute(to_north, "lat", [(i, j) for i, j in swaps if i > j])

    early_rows = EARLY * HALO_SLABS + 32
    early = pl.pallas_call(
        early_kernel,
        out_shape=shape(early_rows, chans),
        in_specs=[vmem] * 2,
        out_specs=vmem,
        scratch_shapes=[pltpu.VMEM((ROWS + 16, chans), F32)],
        compiler_params=pltpu.CompilerParams(vmem_limit_bytes=4 << 20),
        name="early",
    )(own, edge)
    got_early = lax.ppermute(early, "lon", partners("lon", 1, True))

    band, col, lon_a, lon_b = pl.pallas_call(
        band_kernel,
        out_shape=(
            shape(SLABS, EXT, chans),
            shape(64, chans),
            shape(lon_rows, chans),
            shape(LATE * HALO_SLABS + 32, chans),
        ),
        in_specs=[vmem] * 6,
        out_specs=[vmem] * 4,
        scratch_shapes=[
            pltpu.VMEM((lat_rows, chans), BF16),
            pltpu.VMEM((lat_rows, chans), BF16),
            pltpu.VMEM((2, SLABS, 16, chans), F32),
            pltpu.VMEM((64, chans), F32),
        ],
        compiler_params=pltpu.CompilerParams(vmem_limit_bytes=10 << 20),
        name="band",
    )(own, below, edge, got_down, got_a, got_up)

    got_b = lax.ppermute(lon_b, "lon", partners("lon", 1, True))
    count = lax.axis_size("lon")
    chips = [[i, i + 1] for i in range(0, count, 2)]
    both = lax.all_gather(lon_a, "lon", axis_index_groups=chips)

    scratch = [
        pltpu.VMEM(w_two.shape, BF16),
        pltpu.SemaphoreType.DMA,
        pltpu.VMEM((64, chans), F32),
        pltpu.VMEM((2, EXT, LANES), F32),
        pltpu.VMEM((2 * HALO_SLABS, EXT, chans), BF16),
        pltpu.VMEM((SIDE, HID, MAIN), BF16),
        pltpu.VMEM((SIDE, OWN, 3 * PAD), BF16),
    ]
    w_two, b_one = in_hbm(w_two), b_one[None]
    flops = 2 * SIDE * HID * 9 * chans * out_ch + 2 * 6 * OWN * 3 * out_ch * out_ch
    cost = pl.CostEstimate(flops=flops, bytes_accessed=4 << 20, transcendentals=SIDE * HID * out_ch)
    near, w1_main, w1_rest, w2_rest = pl.pallas_call(
        near_kernel,
        out_shape=(
            shape(SLABS, OWN, out_ch, dtype=F32),
            shape(3, 3, chans, MAIN),
            shape(3, chans, MAIN),
            shape(3, 3 * PAD, out_ch),
        ),
        in_specs=[vmem] * 5 + [hbm, vmem],
        out_specs=[vmem] * 4,
        scratch_shapes=scratch + [pltpu.VMEM((3, MAIN, chans), BF16)],
        compiler_params=pltpu.CompilerParams(vmem_limit_bytes=14 << 20),
        cost_estimate=cost,
        name="near_half",
    )(band, col, both, w_one.transpose(0, 1, 3, 2), b_one, w_two, b_two[None])

    return pl.pallas_call(
        far_kernel,
        out_shape=shape(ROWS, COLS, out_ch, dtype=F32),
        in_specs=[vmem] * 7 + [hbm, vmem, vmem, vmem],
        out_specs=vmem,
        scratch_shapes=scratch
        + [pltpu.VMEM((lon_rows, chans), BF16), pltpu.VMEM((64, chans), F32)],
        compiler_params=pltpu.CompilerParams(vmem_limit_bytes=14 << 20),
        cost_estimate=cost,
        name="far_half",
    )(band, col, got_early, got_b, w1_main, w1_rest, b_one, w_two, near, keep, w2_rest)


def solution(mesh):
    return jax.shard_map(
        on_device,
        mesh=mesh,
        in_specs=(P("lat", "lon", None), P("lat", "lon"), P(), P(), P(), P(), P(), P()),
        out_specs=P("lat", "lon", None),
        check_vma=False,
    )
```
